256 devices in a mesh: seq: 32 (over x, z), head: 8 (over y, core).
Axes of the slice: x: 4, y: 4, z: 8, core: 2. Of those that a mesh axis runs over, the one named last changes fastest.
Arguments:
- tokens: bfloat16 [16384, 4096], P('seq'), may hold values from -6 to 6
- w_xz: bfloat16 [4096, 2, 4096], P('seq', None, 'head'), may hold values from -0.09375 to 0.09375
- w_bc: bfloat16 [4096, 256], P('seq'), may hold values from -0.09375 to 0.09375
- conv_x: float32 [4, 4096], P(None, 'head'), may hold values from -3 to 3
- conv_bc: float32 [4, 256], replicated, may hold values from -3 to 3
- tail_x: bfloat16 [3, 4096], P(None, 'head'), may hold values from -6 to 6
- tail_bc: bfloat16 [3, 256], replicated, may hold values from -6 to 6
- decay_code: int32 [16384, 64], P('seq', 'head'), may hold values from 0 to 196608, as said below
- skip_gain: float32 [64], P('head'), may hold values from 0.5 to 2
- state_in: float32 [64, 64, 128], P('head'), may hold values from -180 to 180
- norm_gain: float32 [4096], P('head'), may hold values from 0.1 to 1.9
- w_out: bfloat16 [4096, 4096], P('head', 'seq'), may hold values from -0.1875 to 0.1875
Outputs:
- mixed: bfloat16 [16384, 4096], P('seq', 'head')
The draws below stay inside these ranges and needn't reach their ends.
Inputs may be any that keep to these rules, and one draw needn't show every extreme that they name: `decay_code`: the decay factor of a token and head is exp(-code / 262144).
All inputs are finite; a program needn't handle non-finite values.
Results may differ from the reference program's by a relative error of at most 0.0085.
Values may be sent and summed in bfloat16 or wider, within the bound.
A program may use at most 128 MiB of HBM per device.

```python
import jax
import jax.numpy as jnp
from jax import lax

D = 4096
PARTIAL_SSM_UNIT = 64
P_SIZE = 64
NS = 128
KW = 4
Q = 256
INNER = 4096
SPAN_ENTRIES = 16384


def draw_decay_code(key, part):
    category_entropy_seed, leisurely_entropy_seed, quicker_entropy_seed, spell_entropy_seed, extent_entropy_seed, horizontal_entropy_seed, vertical_entropy_seed = jax.random.split(jax.random.fold_in(key, 11), 7)
    fast = jax.random.randint(category_entropy_seed, (1, PARTIAL_SSM_UNIT), 0, 5) < 2
    slow = jax.random.randint(leisurely_entropy_seed, (SPAN_ENTRIES, PARTIAL_SSM_UNIT), 0, 4)
    quick = jax.random.randint(quicker_entropy_seed, (SPAN_ENTRIES, PARTIAL_SSM_UNIT), 3 * SPAN_ENTRIES // 10, 6 * SPAN_ENTRIES // 10)
    matched_indicator = jax.random.randint(spell_entropy_seed, (SPAN_ENTRIES, PARTIAL_SSM_UNIT), 0, 2048) == 0
    spell_duration = jax.random.randint(extent_entropy_seed, (SPAN_ENTRIES, PARTIAL_SSM_UNIT), 4 * SPAN_ENTRIES, 11 * SPAN_ENTRIES)
    starting_level = jnp.where(fast, quick, slow)
    symbol_entries = jnp.where(matched_indicator, starting_level + spell_duration, starting_level)
    top_row = jax.random.randint(horizontal_entropy_seed, (), 0, SPAN_ENTRIES)
    top_col = jax.random.randint(vertical_entropy_seed, (), 0, PARTIAL_SSM_UNIT)
    places = (jnp.arange(SPAN_ENTRIES)[:, None] == top_row) & (jnp.arange(PARTIAL_SSM_UNIT)[None, :] == top_col)
    return jnp.where(places, 12 * SPAN_ENTRIES, symbol_entries).astype(jnp.int32)


def with_spikes(drawn, stream_key, source, target, blocks, factor):
    owner, partner = [(jnp.arange(drawn.shape[dim]) // (drawn.shape[dim] // blocks)).reshape([-1 if axis == dim else 1 for axis in range(drawn.ndim)]) for dim in (source, target)]
    chosen = jax.random.permutation(stream_key, blocks)[partner]
    strong = (owner == chosen) | (owner == (partner + blocks // 2) % blocks)
    return jnp.where(strong, factor * drawn, drawn)


def steps_of(own_key, extent, shards, low, largest):
    def one(axis_at, shards_of):
        draws = jax.random.uniform(jax.random.fold_in(jax.random.fold_in(own_key, 6), axis_at), (shards_of,), jnp.float32, low / len(shards), largest / len(shards))
        return jnp.repeat(jnp.exp(draws), extent[axis_at] // shards_of).reshape((-1,) + (1,) * (len(extent) - axis_at - 1))

    level = one(*shards[0])
    for cut in shards[1:]:
        level = level * one(*cut)
    return level


def noise(key, shape, scale, limit, shards=(), held_as=jnp.bfloat16):
    gain = steps_of(key, shape, shards, -0.22, 0.18) if shards else 1.0
    values = jax.random.normal(key, shape, jnp.float32) * scale * gain
    return jnp.minimum(jnp.maximum(values, -limit), limit).astype(held_as)


def bell_draw_with(key, extent, scale, bound, pieces, heavy, kind=jnp.bfloat16):
    values = scale * jax.random.normal(key, extent, jnp.float32)
    if pieces:
        values = values * steps_of(key, extent, pieces, -0.22, 0.18)
    return jnp.clip(with_spikes(values, jax.random.fold_in(key, 3), *heavy), -bound, bound).astype(kind)


def setup_inputs(seed: int = 0) -> dict:
    key_list = jax.random.split(jax.random.key(seed), 13)
    return {
        "tokens": noise(key_list[0], (SPAN_ENTRIES, D), 1.0, 6.0, ((0, 32),)),
        "w_xz": noise(key_list[1], (D, 2, INNER), D ** -0.5, 0.09375, ((0, 32), (2, 8))),
        "w_bc": noise(key_list[2], (D, 2 * NS), D ** -0.5, 0.09375, ((0, 32),)),
        "conv_x": noise(key_list[3], (KW, INNER), KW ** -0.5, 3.0, ((1, 8),), jnp.float32),
        "conv_bc": noise(key_list[4], (KW, 2 * NS), KW ** -0.5, 3.0, (), jnp.float32),
        "tail_x": noise(key_list[5], (KW - 1, INNER), 1.0, 6.0, ((1, 8),)),
        "tail_bc": noise(key_list[6], (KW - 1, 2 * NS), 1.0, 6.0),
        "decay_code": draw_decay_code(jax.random.fold_in(key_list[12], 71), 0),
        "skip_gain": jnp.clip(0.5 + 1.5 * jax.random.uniform(key_list[8], (PARTIAL_SSM_UNIT,), jnp.float32) ** steps_of(key_list[8], (PARTIAL_SSM_UNIT,), ((0, 8),), -0.2, 0.2), 0.5, 2.0),
        "state_in": noise(key_list[9], (PARTIAL_SSM_UNIT, P_SIZE, NS), 30.0, 180.0, ((0, 8),), jnp.float32),
        "norm_gain": jnp.clip(1.0 + 0.18 * jax.random.normal(key_list[10], (INNER,), jnp.float32), 0.1, 1.9),
        "w_out": bell_draw_with(key_list[11], (INNER, D), INNER ** -0.5, 0.1875, ((0, 8), (1, 32)), (0, 1, 32, 2.75)),
    }


def depthwise(pre, tail, kernel):
    whole = jnp.concatenate([tail, pre], axis=0).astype(jnp.float32)
    length = pre.shape[0]
    total = jnp.zeros((length, pre.shape[1]), jnp.float32)
    for offset in range(kernel.shape[0]):
        total = total + kernel[offset] * whole[offset:offset + length]
    return jax.nn.silu(total).astype(jnp.bfloat16)

def block_step(state, inputs):
    xval, bval, cval, logdec = inputs
    cum = jnp.cumsum(logdec, axis=0)
    span = cum.shape[0]
    places = jnp.arange(span)
    lower = places[:, None] >= places[None, :]
    cumt = cum.T
    diff = cumt[:, :, None] - cumt[:, None, :]
    decay = jnp.where(lower[None], jnp.exp(jnp.where(lower[None], diff, 0.0)), 0.0)
    scores = jnp.dot(cval, bval.T, preferred_element_type=jnp.float32)
    weights = (decay * scores[None]).astype(jnp.bfloat16)
    inner = jnp.einsum('hts,shp->thp', weights.astype(jnp.float32), xval.astype(jnp.float32), precision=lax.Precision.HIGHEST)
    carried = jnp.einsum('tn,hpn->thp', cval.astype(jnp.float32), state, precision=lax.Precision.HIGHEST)
    carried = carried * jnp.exp(cum)[:, :, None]
    tail_decay = jnp.exp(cum[-1][None, :] - cum)
    decayed_b = (tail_decay.T[:, :, None] * bval.astype(jnp.float32)[None]).astype(jnp.bfloat16)
    added = jnp.einsum('hsn,shp->hpn', decayed_b.astype(jnp.float32), xval.astype(jnp.float32), precision=lax.Precision.HIGHEST)
    new_state = jnp.exp(cum[-1])[:, None, None] * state + added
    return (new_state, inner + carried)

def reference(tokens, w_xz, w_bc, conv_x, conv_bc, tail_x, tail_bc, decay_code, skip_gain, state_in, norm_gain, w_out):
    length = tokens.shape[0]
    heads, head_dim, nstate = state_in.shape
    inner = heads * head_dim
    xz = jnp.dot(tokens, w_xz.reshape(tokens.shape[1], 2 * inner), preferred_element_type=jnp.float32)
    x_pre = xz[:, :inner].astype(jnp.bfloat16)
    z_val = xz[:, inner:].astype(jnp.bfloat16)
    bc_pre = jnp.dot(tokens, w_bc, preferred_element_type=jnp.float32).astype(jnp.bfloat16)
    x_conv = depthwise(x_pre, tail_x, conv_x)
    bc_conv = depthwise(bc_pre, tail_bc, conv_bc)
    b_val = bc_conv[:, :nstate]
    c_val = bc_conv[:, nstate:]
    logdec = -decay_code.astype(jnp.float32) / (16.0 * SPAN_ENTRIES)
    blocks = length // Q
    inputs = (x_conv.reshape(blocks, Q, heads, head_dim), b_val.reshape(blocks, Q, nstate), c_val.reshape(blocks, Q, nstate), logdec.reshape(blocks, Q, heads))
    final_state, parts = lax.scan(block_step, state_in, inputs)
    parts = parts.reshape(length, inner)
    y_val = parts / nstate + jnp.repeat(skip_gain, head_dim)[None, :] * x_conv.astype(jnp.float32)
    gated = y_val * jax.nn.silu(z_val.astype(jnp.float32))
    meansq = lax.optimization_barrier(jnp.mean(gated * gated, axis=1, keepdims=True))
    normed = (gated * lax.rsqrt(meansq + 1e-05) * norm_gain[None, :]).astype(jnp.bfloat16)
    return jnp.dot(normed, w_out, preferred_element_type=jnp.float32).astype(jnp.bfloat16)
```

```python
import jax
import jax.numpy as jnp
from jax import lax
from jax.sharding import PartitionSpec as P

Q = 256


def passed_along(value, axis, by):
    size = lax.axis_size(axis)
    pairs = [(i, i + by) for i in range(size) if 0 <= i + by < size]
    return lax.ppermute(value, axis, pairs)


def depthwise(pre, tail, kernel):
    whole = jnp.concatenate([tail, pre], axis=0).astype(jnp.float32)
    length = pre.shape[0]
    total = jnp.zeros((length, pre.shape[1]), jnp.float32)
    for offset in range(kernel.shape[0]):
        total = total + kernel[offset] * whole[offset : offset + length]
    return jax.nn.silu(total).astype(jnp.bfloat16)


def entering_state(decay, end_state, state_in):
    count = lax.axis_size("seq")
    me = lax.axis_index("seq")
    first = me == 0
    got_a, got_s = passed_along((decay, end_state), "seq", 1)
    acc_a = jnp.where(first, jnp.zeros_like(decay), got_a)
    acc_s = jnp.where(first, state_in, got_s)
    step = 1
    while step < count:
        far_a, far_s = passed_along((acc_a, acc_s), "seq", step)
        has = me >= step
        acc_s = jnp.where(has, acc_a[:, None, None] * far_s + acc_s, acc_s)
        acc_a = jnp.where(has, acc_a * far_a, acc_a)
        step *= 2
    return acc_s


def local(
    tokens,
    w_xz,
    w_bc,
    conv_x,
    conv_bc,
    tail_x,
    tail_bc,
    decay_code,
    skip_gain,
    state_in,
    norm_gain,
    w_out,
):
    rows = tokens.shape[0]
    heads, head_dim, nstate = state_in.shape
    inner = heads * head_dim
    seq_count = lax.axis_size("seq")
    first = lax.axis_index("seq") == 0
    pieces = (
        lax.all_gather(w_xz, "seq", axis=0, tiled=True),
        lax.all_gather(w_bc, "seq", axis=0, tiled=True),
    )
    count = pieces[0].shape[0]
    xz = jnp.dot(tokens, pieces[0].reshape(count, 2 * inner), preferred_element_type=jnp.float32)
    bc_sum = jnp.dot(tokens, pieces[1], preferred_element_type=jnp.float32)
    x_pre = xz[:, :inner].astype(jnp.bfloat16)
    z_val = xz[:, inner:].astype(jnp.bfloat16)
    bc_pre = bc_sum.astype(jnp.bfloat16)
    lag = conv_x.shape[0] - 1
    before_x, before_bc = passed_along((x_pre[rows - lag :], bc_pre[rows - lag :]), "seq", 1)
    before_x = jnp.where(first, tail_x, before_x)
    before_bc = jnp.where(first, tail_bc, before_bc)
    x_conv = depthwise(x_pre, before_x, conv_x)
    bc_conv = depthwise(bc_pre, before_bc, conv_bc)
    b_val = bc_conv[:, :nstate]
    c_val = bc_conv[:, nstate:]
    logdec = -decay_code.astype(jnp.float32) / (16.0 * rows * seq_count)
    blocks = rows // Q
    xb = x_conv.reshape(blocks, Q, heads, head_dim)
    bb = b_val.reshape(blocks, Q, nstate)
    cb = c_val.reshape(blocks, Q, nstate)
    cum = jnp.cumsum(logdec.reshape(blocks, Q, heads), axis=1)

    tail_decay = jnp.exp(cum[:, -1:, :] - cum)
    decayed_b = (
        jnp.transpose(tail_decay, (0, 2, 1))[..., None] * bb.astype(jnp.float32)[:, None]
    ).astype(jnp.bfloat16)
    added = jnp.einsum("bhsn,bshp->bhpn", decayed_b, xb, preferred_element_type=jnp.float32)
    block_decay = jnp.exp(cum[:, -1, :])
    before = [None]
    running = added[0]
    for b in range(1, blocks):
        before.append(running)
        running = block_decay[b][:, None, None] * running + added[b]
    cum_range = jnp.cumsum(logdec, axis=0)
    range_decay = jnp.exp(cum_range[-1])
    incoming = entering_state(range_decay, running, state_in)

    places = jnp.arange(Q)
    lower = places[:, None] >= places[None, :]
    cumt = jnp.transpose(cum, (0, 2, 1))
    diff = cumt[:, :, :, None] - cumt[:, :, None, :]
    decay = jnp.where(lower, jnp.exp(jnp.where(lower, diff, 0.0)), 0.0)
    scores = jnp.einsum("btn,bsn->bts", cb, bb, preferred_element_type=jnp.float32)
    weights = (decay * scores[:, None]).astype(jnp.bfloat16)
    parts = jnp.einsum("bhts,bshp->bthp", weights, xb, preferred_element_type=jnp.float32)
    pieces_out = [parts[0]]
    for b in range(1, blocks):
        carried = jnp.einsum(
            "tn,hpn->thp", cb[b].astype(jnp.float32), before[b], precision=lax.Precision.HIGHEST
        )
        pieces_out.append(parts[b] + carried * jnp.exp(cum[b])[:, :, None])
    parts = jnp.concatenate(pieces_out, axis=0)

    correction = jnp.einsum(
        "tn,hpn->thp", c_val.astype(jnp.float32), incoming, precision=lax.Precision.HIGHEST
    )
    parts = (parts + correction * jnp.exp(cum_range)[:, :, None]).reshape(rows, inner)
    y_val = parts / nstate + jnp.repeat(skip_gain, head_dim)[None, :] * x_conv.astype(jnp.float32)
    gated = y_val * jax.nn.silu(z_val.astype(jnp.float32))
    total_sq = lax.psum(jnp.sum(gated * gated, axis=1), "head")
    meansq = total_sq / (inner * lax.axis_size("head"))
    normed = (gated * lax.rsqrt(meansq[:, None] + 1e-05) * norm_gain[None, :]).astype(jnp.bfloat16)
    partial_out = jnp.dot(
        normed, lax.all_gather(w_out, "seq", axis=1, tiled=True), preferred_element_type=jnp.float32
    )
    result = lax.psum_scatter(partial_out, "head", scatter_dimension=1, tiled=True)
    return result.astype(jnp.bfloat16)


def solution(mesh):
    return jax.shard_map(
        local,
        mesh=mesh,
        in_specs=(
            P("seq", None),
            P("seq", None, "head"),
            P("seq", None),
            P(None, "head"),
            P(),
            P(None, "head"),
            P(),
            P("seq", "head"),
            P("head"),
            P("head", None, None),
            P("head"),
            P("head", "seq"),
        ),
        out_specs=P("seq", "head"),
        check_vma=False,
    )
```

```python
import jax
import jax.numpy as jnp
from jax import lax
from jax.sharding import PartitionSpec as P

Q = 256


def passed_along(value, axis, by):
    size = lax.axis_size(axis)
    pairs = [(i, i + by) for i in range(size) if 0 <= i + by < size]
    return lax.ppermute(value, axis, pairs)


def depthwise(pre, tail, kernel):
    whole = jnp.concatenate([tail, pre], axis=0).astype(jnp.float32)
    length = pre.shape[0]
    total = jnp.zeros((length, pre.shape[1]), jnp.float32)
    for offset in range(kernel.shape[0]):
        total = total + kernel[offset] * whole[offset : offset + length]
    return jax.nn.silu(total).astype(jnp.bfloat16)


def entering_state(decay, end_state, state_in):
    count = lax.axis_size("seq")
    me = lax.axis_index("seq")
    first = me == 0
    lanes = end_state.shape[2]

    def pack(a, s):
        return jnp.concatenate([s, jnp.broadcast_to(a[:, None, None], (a.shape[0], 1, lanes))], axis=1)

    got = passed_along(pack(decay, end_state), "seq", 1)
    acc_a = jnp.where(first, jnp.zeros_like(decay), got[:, -1, 0])
    acc_s = jnp.where(first, state_in, got[:, :-1])
    step = 1
    while step < count:
        far = passed_along(pack(acc_a, acc_s), "seq", step)
        has = me >= step
        acc_s = jnp.where(has, acc_a[:, None, None] * far[:, :-1] + acc_s, acc_s)
        acc_a = jnp.where(has, acc_a * far[:, -1, 0], acc_a)
        step *= 2
    return acc_s


def local(
    tokens,
    w_xz,
    w_bc,
    conv_x,
    conv_bc,
    tail_x,
    tail_bc,
    decay_code,
    skip_gain,
    state_in,
    norm_gain,
    w_out,
):
    rows = tokens.shape[0]
    heads, head_dim, nstate = state_in.shape
    inner = heads * head_dim
    seq_count = lax.axis_size("seq")
    first = lax.axis_index("seq") == 0
    w_x = w_xz[:, 0, :]
    w_z = w_xz[:, 1, :]
    w_out_t = jnp.transpose(w_out)
    widths = (w_x.shape[1], w_z.shape[1], w_bc.shape[1], w_out_t.shape[1])
    packed = jnp.concatenate([w_x, w_z, w_bc, w_out_t], axis=1)
    gathered = lax.all_gather(packed, "seq", axis=0, tiled=True)
    proj = widths[0] + widths[1] + widths[2]
    xzbc = jnp.dot(tokens, gathered[:, :proj], preferred_element_type=jnp.float32)
    w_out_cols = gathered[:, proj:]
    xz = xzbc[:, : 2 * inner]
    bc_sum = xzbc[:, 2 * inner :]
    x_pre = xz[:, :inner].astype(jnp.bfloat16)
    z_val = xz[:, inner:].astype(jnp.bfloat16)
    bc_pre = bc_sum.astype(jnp.bfloat16)
    lag = conv_x.shape[0] - 1
    before_x, before_bc = passed_along((x_pre[rows - lag :], bc_pre[rows - lag :]), "seq", 1)
    before_x = jnp.where(first, tail_x, before_x)
    before_bc = jnp.where(first, tail_bc, before_bc)
    x_conv = depthwise(x_pre, before_x, conv_x)
    bc_conv = depthwise(bc_pre, before_bc, conv_bc)
    b_val = bc_conv[:, :nstate]
    c_val = bc_conv[:, nstate:]
    logdec = -decay_code.astype(jnp.float32) / (16.0 * rows * seq_count)
    blocks = rows // Q
    xb = x_conv.reshape(blocks, Q, heads, head_dim)
    bb = b_val.reshape(blocks, Q, nstate)
    cb = c_val.reshape(blocks, Q, nstate)
    cum = jnp.cumsum(logdec.reshape(blocks, Q, heads), axis=1)

    tail_decay = jnp.exp(cum[:, -1:, :] - cum)
    decayed_b = (
        jnp.transpose(tail_decay, (0, 2, 1))[..., None] * bb.astype(jnp.float32)[:, None]
    ).astype(jnp.bfloat16)
    added = jnp.einsum("bhsn,bshp->bhpn", decayed_b, xb, preferred_element_type=jnp.float32)
    block_decay = jnp.exp(cum[:, -1, :])
    before = [None]
    running = added[0]
    for b in range(1, blocks):
        before.append(running)
        running = block_decay[b][:, None, None] * running + added[b]
    cum_range = jnp.cumsum(logdec, axis=0)
    range_decay = jnp.exp(cum_range[-1])
    incoming = entering_state(range_decay, running, state_in)

    places = jnp.arange(Q)
    lower = places[:, None] >= places[None, :]
    cumt = jnp.transpose(cum, (0, 2, 1))
    diff = cumt[:, :, :, None] - cumt[:, :, None, :]
    decay = jnp.where(lower, jnp.exp(jnp.where(lower, diff, 0.0)), 0.0)
    scores = jnp.einsum("btn,bsn->bts", cb, bb, preferred_element_type=jnp.float32)
    weights = (decay * scores[:, None]).astype(jnp.bfloat16)
    parts = jnp.einsum("bhts,bshp->bthp", weights, xb, preferred_element_type=jnp.float32)
    pieces_out = [parts[0]]
    for b in range(1, blocks):
        carried = jnp.einsum(
            "tn,hpn->thp", cb[b].astype(jnp.float32), before[b], precision=lax.Precision.HIGHEST
        )
        pieces_out.append(parts[b] + carried * jnp.exp(cum[b])[:, :, None])
    parts = jnp.concatenate(pieces_out, axis=0)

    correction = jnp.einsum(
        "tn,hpn->thp", c_val.astype(jnp.float32), incoming, precision=lax.Precision.HIGHEST
    )
    parts = (parts + correction * jnp.exp(cum_range)[:, :, None]).reshape(rows, inner)
    y_val = parts / nstate + jnp.repeat(skip_gain, head_dim)[None, :] * x_conv.astype(jnp.float32)
    gated = y_val * jax.nn.silu(z_val.astype(jnp.float32))
    total_sq = lax.psum(jnp.sum(gated * gated, axis=1), "head")
    meansq = total_sq / (inner * lax.axis_size("head"))
    normed = (gated * lax.rsqrt(meansq[:, None] + 1e-05) * norm_gain[None, :]).astype(jnp.bfloat16)
    partial_out = lax.dot_general(
        normed, w_out_cols, (((1,), (1,)), ((), ())), preferred_element_type=jnp.float32
    )
    result = lax.psum_scatter(partial_out, "head", scatter_dimension=1, tiled=True)
    return result.astype(jnp.bfloat16)


def solution(mesh):
    return jax.shard_map(
        local,
        mesh=mesh,
        in_specs=(
            P("seq", None),
            P("seq", None, "head"),
            P("seq", None),
            P(None, "head"),
            P(),
            P(None, "head"),
            P(),
            P("seq", "head"),
            P("head"),
            P("head", None, None),
            P("head"),
            P("head", "seq"),
        ),
        out_specs=P("seq", "head"),
        check_vma=False,
    )
```

```python
import jax
import jax.numpy as jnp
from jax import lax
from jax.sharding import PartitionSpec as P

Q = 256


def passed_along(value, axis, by):
    size = lax.axis_size(axis)
    pairs = [(i, i + by) for i in range(size) if 0 <= i + by < size]
    return lax.ppermute(value, axis, pairs)


def depthwise(pre, tail, kernel):
    whole = jnp.concatenate([tail, pre], axis=0).astype(jnp.float32)
    length = pre.shape[0]
    total = jnp.zeros((length, pre.shape[1]), jnp.float32)
    for offset in range(kernel.shape[0]):
        total = total + kernel[offset] * whole[offset : offset + length]
    return jax.nn.silu(total).astype(jnp.bfloat16)


def compose(later, earlier):
    return later[0] * earlier[0], later[0][:, None, None] * earlier[1] + later[1]


def entering_state(decay, end_state, state_in):
    count = lax.axis_size("seq")
    me = lax.axis_index("seq")
    lanes = end_state.shape[2]
    ones = jnp.ones_like(decay)
    zeros = jnp.zeros_like(end_state)

    def pack(a, s):
        return jnp.concatenate([s, jnp.broadcast_to(a[:, None, None], (a.shape[0], 1, lanes))], axis=1)

    def unpack(m):
        return m[:, -1, 0], m[:, :-1]

    message = pack(decay, end_state)
    width = min(4, count)
    got = [unpack(passed_along(message, "seq", k)) for k in range(1, width + 1)]
    acc = (ones, zeros)
    for k in range(width, 0, -1):
        src = me - k
        ga = jnp.where(src >= 0, got[k - 1][0], jnp.where(src == -1, 0.0, 1.0))
        gs = jnp.where(src >= 0, got[k - 1][1], jnp.where(src == -1, state_in, zeros))
        acc = compose((ga, gs), acc)
    span = width
    while span < count:
        radix = min(4, -(-count // span))
        message = pack(*acc)
        got = [unpack(passed_along(message, "seq", m * span)) for m in range(1, radix)]
        for m in range(1, radix):
            valid = me - m * span >= 0
            piece = (jnp.where(valid, got[m - 1][0], ones), jnp.where(valid, got[m - 1][1], zeros))
            acc = compose(acc, piece)
        span *= radix
    return acc[1]


def local(
    tokens,
    w_xz,
    w_bc,
    conv_x,
    conv_bc,
    tail_x,
    tail_bc,
    decay_code,
    skip_gain,
    state_in,
    norm_gain,
    w_out,
):
    rows = tokens.shape[0]
    heads, head_dim, nstate = state_in.shape
    inner = heads * head_dim
    seq_count = lax.axis_size("seq")
    first = lax.axis_index("seq") == 0
    w_x = w_xz[:, 0, :]
    w_z = w_xz[:, 1, :]
    w_out_t = jnp.transpose(w_out)
    widths = (w_x.shape[1], w_z.shape[1], w_bc.shape[1], w_out_t.shape[1])
    packed = jnp.concatenate([w_x, w_z, w_bc, w_out_t], axis=1)
    gathered = lax.all_gather(packed, "seq", axis=0, tiled=True)
    proj = widths[0] + widths[1] + widths[2]
    xzbc = jnp.dot(tokens, gathered[:, :proj], preferred_element_type=jnp.float32)
    w_out_cols = gathered[:, proj:]
    xz = xzbc[:, : 2 * inner]
    bc_sum = xzbc[:, 2 * inner :]
    x_pre = xz[:, :inner].astype(jnp.bfloat16)
    z_val = xz[:, inner:].astype(jnp.bfloat16)
    bc_pre = bc_sum.astype(jnp.bfloat16)
    lag = conv_x.shape[0] - 1
    before_x, before_bc = passed_along((x_pre[rows - lag :], bc_pre[rows - lag :]), "seq", 1)
    before_x = jnp.where(first, tail_x, before_x)
    before_bc = jnp.where(first, tail_bc, before_bc)
    x_conv = depthwise(x_pre, before_x, conv_x)
    bc_conv = depthwise(bc_pre, before_bc, conv_bc)
    b_val = bc_conv[:, :nstate]
    c_val = bc_conv[:, nstate:]
    logdec = -decay_code.astype(jnp.float32) / (16.0 * rows * seq_count)
    blocks = rows // Q
    xb = x_conv.reshape(blocks, Q, heads, head_dim)
    bb = b_val.reshape(blocks, Q, nstate)
    cb = c_val.reshape(blocks, Q, nstate)
    cum = jnp.cumsum(logdec.reshape(blocks, Q, heads), axis=1)

    tail_decay = jnp.exp(cum[:, -1:, :] - cum)
    decayed_b = (
        jnp.transpose(tail_decay, (0, 2, 1))[..., None] * bb.astype(jnp.float32)[:, None]
    ).astype(jnp.bfloat16)
    added = jnp.einsum("bhsn,bshp->bhpn", decayed_b, xb, preferred_element_type=jnp.float32)
    block_decay = jnp.exp(cum[:, -1, :])
    before = [None]
    running = added[0]
    for b in range(1, blocks):
        before.append(running)
        running = block_decay[b][:, None, None] * running + added[b]
    cum_range = jnp.cumsum(logdec, axis=0)
    range_decay = jnp.exp(cum_range[-1])
    incoming = entering_state(range_decay, running, state_in)

    places = jnp.arange(Q)
    lower = places[:, None] >= places[None, :]
    cumt = jnp.transpose(cum, (0, 2, 1))
    diff = cumt[:, :, :, None] - cumt[:, :, None, :]
    decay = jnp.where(lower, jnp.exp(jnp.where(lower, diff, 0.0)), 0.0)
    scores = jnp.einsum("btn,bsn->bts", cb, bb, preferred_element_type=jnp.float32)
    weights = (decay * scores[:, None]).astype(jnp.bfloat16)
    parts = jnp.einsum("bhts,bshp->bthp", weights, xb, preferred_element_type=jnp.float32)
    pieces_out = [parts[0]]
    for b in range(1, blocks):
        carried = jnp.einsum(
            "tn,hpn->thp", cb[b].astype(jnp.float32), before[b], precision=lax.Precision.HIGHEST
        )
        pieces_out.append(parts[b] + carried * jnp.exp(cum[b])[:, :, None])
    parts = jnp.concatenate(pieces_out, axis=0)

    correction = jnp.einsum(
        "tn,hpn->thp", c_val.astype(jnp.float32), incoming, precision=lax.Precision.HIGHEST
    )
    parts = (parts + correction * jnp.exp(cum_range)[:, :, None]).reshape(rows, inner)
    y_val = parts / nstate + jnp.repeat(skip_gain, head_dim)[None, :] * x_conv.astype(jnp.float32)
    gated = y_val * jax.nn.silu(z_val.astype(jnp.float32))
    scaled = (gated * norm_gain[None, :]).astype(jnp.bfloat16)
    partial_out = lax.dot_general(
        scaled, w_out_cols, (((1,), (1,)), ((), ())), preferred_element_type=jnp.float32
    )
    result = lax.psum_scatter(partial_out, "head", scatter_dimension=1, tiled=True)
    total_sq = lax.psum(jnp.sum(gated * gated, axis=1), "head")
    meansq = total_sq / (inner * lax.axis_size("head"))
    return (result * lax.rsqrt(meansq[:, None] + 1e-05)).astype(jnp.bfloat16)


def solution(mesh):
    return jax.shard_map(
        local,
        mesh=mesh,
        in_specs=(
            P("seq", None),
            P("seq", None, "head"),
            P("seq", None),
            P(None, "head"),
            P(),
            P(None, "head"),
            P(),
            P("seq", "head"),
            P("head"),
            P("head", None, None),
            P("head"),
            P("head", "seq"),
        ),
        out_specs=P("seq", "head"),
        check_vma=False,
    )
```

```python
import functools

import jax
import jax.numpy as jnp
from jax import lax
from jax.experimental import pallas as pl
from jax.experimental.pallas import tpu as pltpu
from jax.sharding import PartitionSpec as P

Q = 256


def passed_along(value, axis, by):
    size = lax.axis_size(axis)
    pairs = [(i, i + by) for i in range(size) if 0 <= i + by < size]
    return lax.ppermute(value, axis, pairs)


def depthwise(pre, tail, kernel):
    whole = jnp.concatenate([tail, pre], axis=0).astype(jnp.float32)
    length = pre.shape[0]
    total = jnp.zeros((length, pre.shape[1]), jnp.float32)
    for offset in range(kernel.shape[0]):
        total = total + kernel[offset] * whole[offset : offset + length]
    return jax.nn.silu(total).astype(jnp.bfloat16)


def scan_kernel(count, shifts, msg_ref, sin_ref, out_ref, sbuf, rbuf, send_sem, recv_sem):
    me = lax.axis_index("seq")
    hd = lax.axis_index("head")
    rows = sin_ref.shape[1]
    barrier = pltpu.get_barrier_semaphore()
    distinct = sorted(set(shifts))
    for d in distinct:
        for peer in ((me + d) % count, (me + count - d) % count):
            pl.semaphore_signal(barrier, inc=1, device_id=(peer, hd), device_id_type=pl.DeviceIdType.MESH)
    pl.semaphore_wait(barrier, 2 * len(distinct))
    copies = []
    for k, d in enumerate(shifts):
        if k == 0:
            sbuf[k] = msg_ref[...]
        else:
            sbuf[k] = out_ref[...]
        copy = pltpu.make_async_remote_copy(
            src_ref=sbuf.at[k],
            dst_ref=rbuf.at[k],
            send_sem=send_sem.at[k],
            recv_sem=recv_sem.at[k],
            device_id=((me + d) % count, hd),
            device_id_type=pl.DeviceIdType.MESH,
        )
        copy.start()
        copies.append(copy)
        copy.wait_recv()
        far = rbuf[k]
        if k == 0:
            opening = jnp.concatenate(
                [sin_ref[...], jnp.zeros((far.shape[0], far.shape[1] - rows, far.shape[2]), far.dtype)], axis=1
            )
            out_ref[...] = jnp.where(me == 0, opening, far)
        else:
            acc = out_ref[...]
            acc_a = acc[:, rows:, :]
            acc_a_rows = jnp.tile(acc_a, (1, rows // acc_a.shape[1], 1))
            new_s = acc_a_rows * far[:, :rows, :] + acc[:, :rows, :]
            new_a = acc_a * far[:, rows:, :]
            combined = jnp.concatenate([new_s, new_a], axis=1)
            out_ref[...] = jnp.where(me >= d, combined, acc)
    for copy in copies:
        copy.wait_send()


def entering_state(decay, end_state, state_in):
    count = lax.axis_size("seq")
    heads, rows, lanes = end_state.shape
    pad = 8
    message = jnp.concatenate([end_state, jnp.broadcast_to(decay[:, None, None], (heads, pad, lanes))], axis=1)
    shifts = [1]
    step = 1
    while step < count:
        shifts.append(step)
        step *= 2
    shape = message.shape
    out = pl.pallas_call(
        functools.partial(scan_kernel, count, tuple(shifts)),
        out_shape=jax.ShapeDtypeStruct(shape, jnp.float32),
        in_specs=[pl.BlockSpec(memory_space=pltpu.VMEM)] * 2,
        out_specs=pl.BlockSpec(memory_space=pltpu.VMEM),
        scratch_shapes=[
            pltpu.VMEM((len(shifts),) + shape, jnp.float32),
            pltpu.VMEM((len(shifts),) + shape, jnp.float32),
            pltpu.SemaphoreType.DMA((len(shifts),)),
            pltpu.SemaphoreType.DMA((len(shifts),)),
        ],
        compiler_params=pltpu.CompilerParams(collective_id=0, has_side_effects=True),
    )(message, state_in)
    return out[:, :rows, :]


def local(
    tokens,
    w_xz,
    w_bc,
    conv_x,
    conv_bc,
    tail_x,
    tail_bc,
    decay_code,
    skip_gain,
    state_in,
    norm_gain,
    w_out,
):
    rows = tokens.shape[0]
    heads, head_dim, nstate = state_in.shape
    inner = heads * head_dim
    seq_count = lax.axis_size("seq")
    first = lax.axis_index("seq") == 0
    w_x = w_xz[:, 0, :]
    w_z = w_xz[:, 1, :]
    w_out_t = jnp.transpose(w_out)
    widths = (w_x.shape[1], w_z.shape[1], w_bc.shape[1], w_out_t.shape[1])
    packed = jnp.concatenate([w_x, w_z, w_bc, w_out_t], axis=1)
    gathered = lax.all_gather(packed, "seq", axis=0, tiled=True)
    proj = widths[0] + widths[1] + widths[2]
    xzbc = jnp.dot(tokens, gathered[:, :proj], preferred_element_type=jnp.float32)
    w_out_cols = gathered[:, proj:]
    xz = xzbc[:, : 2 * inner]
    bc_sum = xzbc[:, 2 * inner :]
    x_pre = xz[:, :inner].astype(jnp.bfloat16)
    z_val = xz[:, inner:].astype(jnp.bfloat16)
    bc_pre = bc_sum.astype(jnp.bfloat16)
    lag = conv_x.shape[0] - 1
    before_x, before_bc = passed_along((x_pre[rows - lag :], bc_pre[rows - lag :]), "seq", 1)
    before_x = jnp.where(first, tail_x, before_x)
    before_bc = jnp.where(first, tail_bc, before_bc)
    x_conv = depthwise(x_pre, before_x, conv_x)
    bc_conv = depthwise(bc_pre, before_bc, conv_bc)
    b_val = bc_conv[:, :nstate]
    c_val = bc_conv[:, nstate:]
    logdec = -decay_code.astype(jnp.float32) / (16.0 * rows * seq_count)
    blocks = rows // Q
    xb = x_conv.reshape(blocks, Q, heads, head_dim)
    bb = b_val.reshape(blocks, Q, nstate)
    cb = c_val.reshape(blocks, Q, nstate)
    cum = jnp.cumsum(logdec.reshape(blocks, Q, heads), axis=1)

    tail_decay = jnp.exp(cum[:, -1:, :] - cum)
    decayed_b = (
        jnp.transpose(tail_decay, (0, 2, 1))[..., None] * bb.astype(jnp.float32)[:, None]
    ).astype(jnp.bfloat16)
    added = jnp.einsum("bhsn,bshp->bhpn", decayed_b, xb, preferred_element_type=jnp.float32)
    block_decay = jnp.exp(cum[:, -1, :])
    before = [None]
    running = added[0]
    for b in range(1, blocks):
        before.append(running)
        running = block_decay[b][:, None, None] * running + added[b]
    cum_range = jnp.cumsum(logdec, axis=0)
    range_decay = jnp.exp(cum_range[-1])
    incoming = entering_state(range_decay, running, state_in)

    places = jnp.arange(Q)
    lower = places[:, None] >= places[None, :]
    cumt = jnp.transpose(cum, (0, 2, 1))
    diff = cumt[:, :, :, None] - cumt[:, :, None, :]
    decay = jnp.where(lower, jnp.exp(jnp.where(lower, diff, 0.0)), 0.0)
    scores = jnp.einsum("btn,bsn->bts", cb, bb, preferred_element_type=jnp.float32)
    weights = (decay * scores[:, None]).astype(jnp.bfloat16)
    parts = jnp.einsum("bhts,bshp->bthp", weights, xb, preferred_element_type=jnp.float32)
    pieces_out = [parts[0]]
    for b in range(1, blocks):
        carried = jnp.einsum(
            "tn,hpn->thp", cb[b].astype(jnp.float32), before[b], precision=lax.Precision.HIGHEST
        )
        pieces_out.append(parts[b] + carried * jnp.exp(cum[b])[:, :, None])
    parts = jnp.concatenate(pieces_out, axis=0)

    correction = jnp.einsum(
        "tn,hpn->thp", c_val.astype(jnp.float32), incoming, precision=lax.Precision.HIGHEST
    )
    parts = (parts + correction * jnp.exp(cum_range)[:, :, None]).reshape(rows, inner)
    y_val = parts / nstate + jnp.repeat(skip_gain, head_dim)[None, :] * x_conv.astype(jnp.float32)
    gated = y_val * jax.nn.silu(z_val.astype(jnp.float32))
    scaled = (gated * norm_gain[None, :]).astype(jnp.bfloat16)
    partial_out = lax.dot_general(
        scaled, w_out_cols, (((1,), (1,)), ((), ())), preferred_element_type=jnp.float32
    )
    result = lax.psum_scatter(partial_out, "head", scatter_dimension=1, tiled=True)
    total_sq = lax.psum(jnp.sum(gated * gated, axis=1), "head")
    meansq = total_sq / (inner * lax.axis_size("head"))
    return (result * lax.rsqrt(meansq[:, None] + 1e-05)).astype(jnp.bfloat16)


def solution(mesh):
    return jax.shard_map(
        local,
        mesh=mesh,
        in_specs=(
            P("seq", None),
            P("seq", None, "head"),
            P("seq", None),
            P(None, "head"),
            P(),
            P(None, "head"),
            P(),
            P("seq", "head"),
            P("head"),
            P("head", None, None),
            P("head"),
            P("head", "seq"),
        ),
        out_specs=P("seq", "head"),
        check_vma=False,
    )
```

```python
import functools

import jax
import jax.numpy as jnp
from jax import lax
from jax.experimental import pallas as pl
from jax.experimental.pallas import tpu as pltpu
from jax.sharding import PartitionSpec as P

Q = 256


def passed_along(value, axis, by):
    size = lax.axis_size(axis)
    pairs = [(i, i + by) for i in range(size) if 0 <= i + by < size]
    return lax.ppermute(value, axis, pairs)


def depthwise(pre, tail, kernel):
    whole = jnp.concatenate([tail, pre], axis=0).astype(jnp.float32)
    length = pre.shape[0]
    total = jnp.zeros((length, pre.shape[1]), jnp.float32)
    for offset in range(kernel.shape[0]):
        total = total + kernel[offset] * whole[offset : offset + length]
    return jax.nn.silu(total).astype(jnp.bfloat16)


def scan_kernel(count, shifts, msg_ref, dec_ref, sin_ref, out_ref, dec_acc, s_send, a_send, s_recv, a_recv, send_sem, recv_sem):
    me = lax.axis_index("seq")
    hd = lax.axis_index("head")
    barrier = pltpu.get_barrier_semaphore()
    distinct = sorted(set(shifts))
    for d in distinct:
        for peer in ((me + d) % count, (me + count - d) % count):
            pl.semaphore_signal(barrier, inc=1, device_id=(peer, hd), device_id_type=pl.DeviceIdType.MESH)
    pl.semaphore_wait(barrier, 2 * len(distinct))
    copies = []
    for k, d in enumerate(shifts):
        if k == 0:
            s_send[k] = msg_ref[...].astype(s_send.dtype)
            a_send[k] = dec_ref[...]
        else:
            s_send[k] = out_ref[...].astype(s_send.dtype)
            a_send[k] = dec_acc[...]
        target = ((me + d) % count, hd)
        pair = []
        for index, (src, dst) in enumerate(((s_send, s_recv), (a_send, a_recv))):
            copy = pltpu.make_async_remote_copy(
                src_ref=src.at[k],
                dst_ref=dst.at[k],
                send_sem=send_sem.at[index, k],
                recv_sem=recv_sem.at[index, k],
                device_id=target,
                device_id_type=pl.DeviceIdType.MESH,
            )
            copy.start()
            pair.append(copy)
        copies.extend(pair)
        for copy in pair:
            copy.wait_recv()
        far_s = s_recv[k].astype(jnp.float32)
        far_a = a_recv[k]
        if k == 0:
            out_ref[...] = jnp.where(me == 0, sin_ref[...], far_s)
            dec_acc[...] = jnp.where(me == 0, jnp.zeros_like(far_a), far_a)
        else:
            acc_s = out_ref[...]
            acc_a = dec_acc[...]
            rows = acc_s.shape[1]
            acc_a_rows = jnp.tile(acc_a, (1, rows // acc_a.shape[1], 1))
            out_ref[...] = jnp.where(me >= d, acc_a_rows * far_s + acc_s, acc_s)
            dec_acc[...] = jnp.where(me >= d, acc_a * far_a, acc_a)
    for copy in copies:
        copy.wait_send()


def entering_state(decay, end_state, state_in):
    count = lax.axis_size("seq")
    heads, rows, lanes = end_state.shape
    decay_rows = jnp.broadcast_to(decay[:, None, None], (heads, 8, lanes))
    shifts = [1]
    step = 1
    while step < count:
        shifts.append(step)
        step *= 2
    steps = len(shifts)
    return pl.pallas_call(
        functools.partial(scan_kernel, count, tuple(shifts)),
        out_shape=jax.ShapeDtypeStruct(end_state.shape, jnp.float32),
        in_specs=[pl.BlockSpec(memory_space=pltpu.VMEM)] * 3,
        out_specs=pl.BlockSpec(memory_space=pltpu.VMEM),
        scratch_shapes=[
            pltpu.VMEM(decay_rows.shape, jnp.float32),
            pltpu.VMEM((steps,) + end_state.shape, jnp.bfloat16),
            pltpu.VMEM((steps,) + decay_rows.shape, jnp.float32),
            pltpu.VMEM((steps,) + end_state.shape, jnp.bfloat16),
            pltpu.VMEM((steps,) + decay_rows.shape, jnp.float32),
            pltpu.SemaphoreType.DMA((2, steps)),
            pltpu.SemaphoreType.DMA((2, steps)),
        ],
        compiler_params=pltpu.CompilerParams(collective_id=0, has_side_effects=True),
    )(end_state, decay_rows, state_in)


def local(
    tokens,
    w_xz,
    w_bc,
    conv_x,
    conv_bc,
    tail_x,
    tail_bc,
    decay_code,
    skip_gain,
    state_in,
    norm_gain,
    w_out,
):
    rows = tokens.shape[0]
    heads, head_dim, nstate = state_in.shape
    inner = heads * head_dim
    seq_count = lax.axis_size("seq")
    first = lax.axis_index("seq") == 0
    w_x = w_xz[:, 0, :]
    w_z = w_xz[:, 1, :]
    packed = jnp.concatenate([w_x, w_z, w_bc], axis=1)
    gathered = lax.all_gather(packed, "seq", axis=0, tiled=True)
    w_out_cols = lax.all_gather(jnp.transpose(w_out), "seq", axis=0, tiled=True)
    xzbc = jnp.dot(tokens, gathered, preferred_element_type=jnp.float32)
    xz = xzbc[:, : 2 * inner]
    bc_sum = xzbc[:, 2 * inner :]
    x_pre = xz[:, :inner].astype(jnp.bfloat16)
    z_val = xz[:, inner:].astype(jnp.bfloat16)
    bc_pre = bc_sum.astype(jnp.bfloat16)
    lag = conv_x.shape[0] - 1
    before_x, before_bc = passed_along((x_pre[rows - lag :], bc_pre[rows - lag :]), "seq", 1)
    before_x = jnp.where(first, tail_x, before_x)
    before_bc = jnp.where(first, tail_bc, before_bc)
    x_conv = depthwise(x_pre, before_x, conv_x)
    bc_conv = depthwise(bc_pre, before_bc, conv_bc)
    b_val = bc_conv[:, :nstate]
    c_val = bc_conv[:, nstate:]
    logdec = -decay_code.astype(jnp.float32) / (16.0 * rows * seq_count)
    blocks = rows // Q
    xb = x_conv.reshape(blocks, Q, heads, head_dim)
    bb = b_val.reshape(blocks, Q, nstate)
    cb = c_val.reshape(blocks, Q, nstate)
    cum = jnp.cumsum(logdec.reshape(blocks, Q, heads), axis=1)

    tail_decay = jnp.exp(cum[:, -1:, :] - cum)
    decayed_b = (
        jnp.transpose(tail_decay, (0, 2, 1))[..., None] * bb.astype(jnp.float32)[:, None]
    ).astype(jnp.bfloat16)
    added = jnp.einsum("bhsn,bshp->bhpn", decayed_b, xb, preferred_element_type=jnp.float32)
    block_decay = jnp.exp(cum[:, -1, :])
    before = [None]
    running = added[0]
    for b in range(1, blocks):
        before.append(running)
        running = block_decay[b][:, None, None] * running + added[b]
    cum_range = jnp.cumsum(logdec, axis=0)
    range_decay = jnp.exp(cum_range[-1])
    incoming = entering_state(range_decay, running, state_in)

    places = jnp.arange(Q)
    lower = places[:, None] >= places[None, :]
    cumt = jnp.transpose(cum, (0, 2, 1))
    diff = cumt[:, :, :, None] - cumt[:, :, None, :]
    decay = jnp.where(lower, jnp.exp(jnp.where(lower, diff, 0.0)), 0.0)
    scores = jnp.einsum("btn,bsn->bts", cb, bb, preferred_element_type=jnp.float32)
    weights = (decay * scores[:, None]).astype(jnp.bfloat16)
    parts = jnp.einsum("bhts,bshp->bthp", weights, xb, preferred_element_type=jnp.float32)
    pieces_out = [parts[0]]
    for b in range(1, blocks):
        carried = jnp.einsum(
            "tn,hpn->thp", cb[b].astype(jnp.float32), before[b], precision=lax.Precision.HIGHEST
        )
        pieces_out.append(parts[b] + carried * jnp.exp(cum[b])[:, :, None])
    parts = jnp.concatenate(pieces_out, axis=0)

    correction = jnp.einsum(
        "tn,hpn->thp", c_val.astype(jnp.float32), incoming, precision=lax.Precision.HIGHEST
    )
    parts = (parts + correction * jnp.exp(cum_range)[:, :, None]).reshape(rows, inner)
    y_val = parts / nstate + jnp.repeat(skip_gain, head_dim)[None, :] * x_conv.astype(jnp.float32)
    gated = y_val * jax.nn.silu(z_val.astype(jnp.float32))
    scaled = (gated * norm_gain[None, :]).astype(jnp.bfloat16)
    partial_out = lax.dot_general(
        scaled, w_out_cols, (((1,), (1,)), ((), ())), preferred_element_type=jnp.float32
    )
    result = lax.psum_scatter(partial_out, "head", scatter_dimension=1, tiled=True)
    total_sq = lax.psum(jnp.sum(gated * gated, axis=1), "head")
    meansq = total_sq / (inner * lax.axis_size("head"))
    return (result * lax.rsqrt(meansq[:, None] + 1e-05)).astype(jnp.bfloat16)


def solution(mesh):
    return jax.shard_map(
        local,
        mesh=mesh,
        in_specs=(
            P("seq", None),
            P("seq", None, "head"),
            P("seq", None),
            P(None, "head"),
            P(),
            P(None, "head"),
            P(),
            P("seq", "head"),
            P("head"),
            P("head", None, None),
            P("head"),
            P("head", "seq"),
        ),
        out_specs=P("seq", "head"),
        check_vma=False,
    )
```

```python
import functools

import jax
import jax.numpy as jnp
from jax import lax
from jax.experimental import pallas as pl
from jax.experimental.pallas import tpu as pltpu
from jax.sharding import PartitionSpec as P

Q = 256


def passed_along(value, axis, by):
    size = lax.axis_size(axis)
    pairs = [(i, i + by) for i in range(size) if 0 <= i + by < size]
    return lax.ppermute(value, axis, pairs)


def depthwise(whole, kernel):
    whole = whole.astype(jnp.float32)
    length = whole.shape[0] - kernel.shape[0] + 1
    total = jnp.zeros((length, whole.shape[1]), jnp.float32)
    for offset in range(kernel.shape[0]):
        total = total + kernel[offset] * whole[offset : offset + length]
    return jax.nn.silu(total).astype(jnp.bfloat16)


def scan_kernel(count, shifts, msg_ref, dec_ref, sin_ref, out_ref, dec_acc, s_send, a_send, s_recv, a_recv, send_sem, recv_sem):
    me = lax.axis_index("seq")
    hd = lax.axis_index("head")
    barrier = pltpu.get_barrier_semaphore()
    distinct = sorted(set(shifts))
    for d in distinct:
        for peer in ((me + d) % count, (me + count - d) % count):
            pl.semaphore_signal(barrier, inc=1, device_id=(peer, hd), device_id_type=pl.DeviceIdType.MESH)
    pl.semaphore_wait(barrier, 2 * len(distinct))
    copies = []
    for k, d in enumerate(shifts):
        if k == 0:
            s_send[k] = msg_ref[...].astype(s_send.dtype)
            a_send[k] = dec_ref[...]
        else:
            s_send[k] = out_ref[...].astype(s_send.dtype)
            a_send[k] = dec_acc[...]
        target = ((me + d) % count, hd)
        pair = []
        for index, (src, dst) in enumerate(((s_send, s_recv), (a_send, a_recv))):
            copy = pltpu.make_async_remote_copy(
                src_ref=src.at[k],
                dst_ref=dst.at[k],
                send_sem=send_sem.at[index, k],
                recv_sem=recv_sem.at[index, k],
                device_id=target,
                device_id_type=pl.DeviceIdType.MESH,
            )
            copy.start()
            pair.append(copy)
        copies.extend(pair)
        for copy in pair:
            copy.wait_recv()
        far_s = s_recv[k].astype(jnp.float32)
        far_a = a_recv[k]
        if k == 0:
            out_ref[...] = jnp.where(me == 0, sin_ref[...], far_s)
            dec_acc[...] = jnp.where(me == 0, jnp.zeros_like(far_a), far_a)
        else:
            acc_s = out_ref[...]
            acc_a = dec_acc[...]
            rows = acc_s.shape[1]
            acc_a_rows = jnp.tile(acc_a, (1, rows // acc_a.shape[1], 1))
            out_ref[...] = jnp.where(me >= d, acc_a_rows * far_s + acc_s, acc_s)
            dec_acc[...] = jnp.where(me >= d, acc_a * far_a, acc_a)
    for copy in copies:
        copy.wait_send()


def entering_state(decay, end_state, state_in):
    count = lax.axis_size("seq")
    heads, rows, lanes = end_state.shape
    decay_rows = jnp.broadcast_to(decay[:, None, None], (heads, 8, lanes))
    shifts = [1]
    step = 1
    while step < count:
        shifts.append(step)
        step *= 2
    steps = len(shifts)
    return pl.pallas_call(
        functools.partial(scan_kernel, count, tuple(shifts)),
        out_shape=jax.ShapeDtypeStruct(end_state.shape, jnp.float32),
        in_specs=[pl.BlockSpec(memory_space=pltpu.VMEM)] * 3,
        out_specs=pl.BlockSpec(memory_space=pltpu.VMEM),
        scratch_shapes=[
            pltpu.VMEM(decay_rows.shape, jnp.float32),
            pltpu.VMEM((steps,) + end_state.shape, jnp.bfloat16),
            pltpu.VMEM((steps,) + decay_rows.shape, jnp.float32),
            pltpu.VMEM((steps,) + end_state.shape, jnp.bfloat16),
            pltpu.VMEM((steps,) + decay_rows.shape, jnp.float32),
            pltpu.SemaphoreType.DMA((2, steps)),
            pltpu.SemaphoreType.DMA((2, steps)),
        ],
        compiler_params=pltpu.CompilerParams(collective_id=0, has_side_effects=True),
    )(end_state, decay_rows, state_in)


def local(
    tokens,
    w_xz,
    w_bc,
    conv_x,
    conv_bc,
    tail_x,
    tail_bc,
    decay_code,
    skip_gain,
    state_in,
    norm_gain,
    w_out,
):
    rows = tokens.shape[0]
    heads, head_dim, nstate = state_in.shape
    inner = heads * head_dim
    seq_count = lax.axis_size("seq")
    first = lax.axis_index("seq") == 0
    w_x = w_xz[:, 0, :]
    w_z = w_xz[:, 1, :]
    packed = jnp.concatenate([w_x, w_z, w_bc], axis=1)
    gathered = lax.all_gather(packed, "seq", axis=0, tiled=True)
    w_out_cols = lax.all_gather(jnp.transpose(w_out), "seq", axis=0, tiled=True)
    lag = conv_x.shape[0] - 1
    earlier = passed_along(tokens[rows - lag :], "seq", 1)
    extended = jnp.concatenate([earlier, tokens], axis=0)
    xzbc = jnp.dot(extended, gathered, preferred_element_type=jnp.float32).astype(jnp.bfloat16)
    opening = lax.broadcasted_iota(jnp.int32, (rows + lag, 1), 0) < lag
    whole_x = jnp.where(first & opening, jnp.pad(tail_x, ((0, rows), (0, 0))), xzbc[:, :inner])
    whole_bc = jnp.where(first & opening, jnp.pad(tail_bc, ((0, rows), (0, 0))), xzbc[:, 2 * inner :])
    z_val = xzbc[lag:, inner : 2 * inner]
    x_conv = depthwise(whole_x, conv_x)
    bc_conv = depthwise(whole_bc, conv_bc)
    b_val = bc_conv[:, :nstate]
    c_val = bc_conv[:, nstate:]
    logdec = -decay_code.astype(jnp.float32) / (16.0 * rows * seq_count)
    blocks = rows // Q
    xb = x_conv.reshape(blocks, Q, heads, head_dim)
    bb = b_val.reshape(blocks, Q, nstate)
    cb = c_val.reshape(blocks, Q, nstate)
    cum = jnp.cumsum(logdec.reshape(blocks, Q, heads), axis=1)

    tail_decay = jnp.exp(cum[:, -1:, :] - cum)
    decayed_b = (
        jnp.transpose(tail_decay, (0, 2, 1))[..., None] * bb.astype(jnp.float32)[:, None]
    ).astype(jnp.bfloat16)
    added = jnp.einsum("bhsn,bshp->bhpn", decayed_b, xb, preferred_element_type=jnp.float32)
    block_decay = jnp.exp(cum[:, -1, :])
    before = [None]
    running = added[0]
    for b in range(1, blocks):
        before.append(running)
        running = block_decay[b][:, None, None] * running + added[b]
    cum_range = jnp.cumsum(logdec, axis=0)
    range_decay = jnp.exp(cum_range[-1])
    incoming = entering_state(range_decay, running, state_in)

    places = jnp.arange(Q)
    lower = places[:, None] >= places[None, :]
    cumt = jnp.transpose(cum, (0, 2, 1))
    diff = cumt[:, :, :, None] - cumt[:, :, None, :]
    decay = jnp.where(lower, jnp.exp(jnp.where(lower, diff, 0.0)), 0.0)
    scores = jnp.einsum("btn,bsn->bts", cb, bb, preferred_element_type=jnp.float32)
    weights = (decay * scores[:, None]).astype(jnp.bfloat16)
    parts = jnp.einsum("bhts,bshp->bthp", weights, xb, preferred_element_type=jnp.float32)
    pieces_out = [parts[0]]
    for b in range(1, blocks):
        carried = jnp.einsum(
            "tn,hpn->thp", cb[b].astype(jnp.float32), before[b], precision=lax.Precision.HIGHEST
        )
        pieces_out.append(parts[b] + carried * jnp.exp(cum[b])[:, :, None])
    parts = jnp.concatenate(pieces_out, axis=0)

    correction = jnp.einsum(
        "tn,hpn->thp", c_val.astype(jnp.float32), incoming, precision=lax.Precision.HIGHEST
    )
    parts = (parts + correction * jnp.exp(cum_range)[:, :, None]).reshape(rows, inner)
    y_val = parts / nstate + jnp.repeat(skip_gain, head_dim)[None, :] * x_conv.astype(jnp.float32)
    gated = y_val * jax.nn.silu(z_val.astype(jnp.float32))
    scaled = (gated * norm_gain[None, :]).astype(jnp.bfloat16)
    partial_out = lax.dot_general(
        scaled, w_out_cols, (((1,), (1,)), ((), ())), preferred_element_type=jnp.float32
    )
    result = lax.psum_scatter(
        partial_out.astype(jnp.bfloat16), "head", scatter_dimension=1, tiled=True
    ).astype(jnp.float32)
    total_sq = lax.psum(jnp.sum(gated * gated, axis=1), "head")
    meansq = total_sq / (inner * lax.axis_size("head"))
    return (result * lax.rsqrt(meansq[:, None] + 1e-05)).astype(jnp.bfloat16)


def solution(mesh):
    return jax.shard_map(
        local,
        mesh=mesh,
        in_specs=(
            P("seq", None),
            P("seq", None, "head"),
            P("seq", None),
            P(None, "head"),
            P(),
            P(None, "head"),
            P(),
            P("seq", "head"),
            P("head"),
            P("head", None, None),
            P("head"),
            P("head", "seq"),
        ),
        out_specs=P("seq", "head"),
        check_vma=False,
    )
```

```python
import functools

import jax
import jax.numpy as jnp
from jax import lax
from jax.experimental import pallas as pl
from jax.experimental.pallas import tpu as pltpu
from jax.sharding import Mesh, PartitionSpec as P

Q = 256


SEQ = ("sx", "sz")


def seq_size():
    return lax.axis_size("sx") * lax.axis_size("sz")


def passed_along(value, axis, by):
    size = seq_size() if axis == SEQ else lax.axis_size(axis)
    pairs = [(i, i + by) for i in range(size) if 0 <= i + by < size]
    return lax.ppermute(value, axis, pairs)


def depthwise(whole, kernel):
    whole = whole.astype(jnp.float32)
    length = whole.shape[0] - kernel.shape[0] + 1
    total = jnp.zeros((length, whole.shape[1]), jnp.float32)
    for offset in range(kernel.shape[0]):
        total = total + kernel[offset] * whole[offset : offset + length]
    return jax.nn.silu(total).astype(jnp.bfloat16)


def scan_kernel(count, minor, shifts, msg_ref, dec_ref, sin_ref, out_ref, dec_acc, s_send, a_send, s_recv, a_recv, send_sem, recv_sem):
    me = lax.axis_index("sx") * minor + lax.axis_index("sz")
    hd = lax.axis_index("head")
    barrier = pltpu.get_barrier_semaphore()
    distinct = sorted(set(shifts))
    for d in distinct:
        for peer in ((me + d) % count, (me + count - d) % count):
            pl.semaphore_signal(
                barrier, inc=1, device_id=(peer // minor, peer % minor, hd), device_id_type=pl.DeviceIdType.MESH
            )
    pl.semaphore_wait(barrier, 2 * len(distinct))
    copies = []
    for k, d in enumerate(shifts):
        if k == 0:
            s_send[k] = msg_ref[...].astype(s_send.dtype)
            a_send[k] = dec_ref[...]
        else:
            s_send[k] = out_ref[...].astype(s_send.dtype)
            a_send[k] = dec_acc[...]
        target = ((me + d) % count // minor, (me + d) % count % minor, hd)
        pair = []
        for index, (src, dst) in enumerate(((s_send, s_recv), (a_send, a_recv))):
            copy = pltpu.make_async_remote_copy(
                src_ref=src.at[k],
                dst_ref=dst.at[k],
                send_sem=send_sem.at[index, k],
                recv_sem=recv_sem.at[index, k],
                device_id=target,
                device_id_type=pl.DeviceIdType.MESH,
            )
            copy.start()
            pair.append(copy)
        copies.extend(pair)
        for copy in pair:
            copy.wait_recv()
        far_s = s_recv[k].astype(jnp.float32)
        far_a = a_recv[k]
        if k == 0:
            out_ref[...] = jnp.where(me == 0, sin_ref[...], far_s)
            dec_acc[...] = jnp.where(me == 0, jnp.zeros_like(far_a), far_a)
        else:
            acc_s = out_ref[...]
            acc_a = dec_acc[...]
            rows = acc_s.shape[1]
            acc_a_rows = jnp.tile(acc_a, (1, rows // acc_a.shape[1], 1))
            out_ref[...] = jnp.where(me >= d, acc_a_rows * far_s + acc_s, acc_s)
            dec_acc[...] = jnp.where(me >= d, acc_a * far_a, acc_a)
    for copy in copies:
        copy.wait_send()


def entering_state(decay, end_state, state_in):
    count = seq_size()
    minor = lax.axis_size("sz")
    heads, rows, lanes = end_state.shape
    decay_rows = jnp.broadcast_to(decay[:, None, None], (heads, 8, lanes))
    shifts = [1]
    step = 1
    while step < count:
        shifts.append(step)
        step *= 2
    steps = len(shifts)
    return pl.pallas_call(
        functools.partial(scan_kernel, count, minor, tuple(shifts)),
        out_shape=jax.ShapeDtypeStruct(end_state.shape, jnp.float32),
        in_specs=[pl.BlockSpec(memory_space=pltpu.VMEM)] * 3,
        out_specs=pl.BlockSpec(memory_space=pltpu.VMEM),
        scratch_shapes=[
            pltpu.VMEM(decay_rows.shape, jnp.float32),
            pltpu.VMEM((steps,) + end_state.shape, jnp.bfloat16),
            pltpu.VMEM((steps,) + decay_rows.shape, jnp.float32),
            pltpu.VMEM((steps,) + end_state.shape, jnp.bfloat16),
            pltpu.VMEM((steps,) + decay_rows.shape, jnp.float32),
            pltpu.SemaphoreType.DMA((2, steps)),
            pltpu.SemaphoreType.DMA((2, steps)),
        ],
        compiler_params=pltpu.CompilerParams(collective_id=0, has_side_effects=True),
    )(end_state, decay_rows, state_in)


def gather_seq(value):
    value = lax.all_gather(value, "sz", axis=0, tiled=True)
    return lax.all_gather(value, "sx", axis=0, tiled=True)


def local(
    tokens,
    w_xz,
    w_bc,
    conv_x,
    conv_bc,
    tail_x,
    tail_bc,
    decay_code,
    skip_gain,
    state_in,
    norm_gain,
    w_out,
):
    rows = tokens.shape[0]
    heads, head_dim, nstate = state_in.shape
    inner = heads * head_dim
    seq_count = seq_size()
    first = lax.axis_index(SEQ) == 0
    w_x = w_xz[:, 0, :]
    w_z = w_xz[:, 1, :]
    packed = jnp.concatenate([w_x, w_z, w_bc], axis=1)
    gathered = gather_seq(packed)
    w_out_cols = gather_seq(jnp.transpose(w_out))
    lag = conv_x.shape[0] - 1
    earlier = passed_along(tokens[rows - lag :], SEQ, 1)
    extended = jnp.concatenate([earlier, tokens], axis=0)
    xzbc = jnp.dot(extended, gathered, preferred_element_type=jnp.float32).astype(jnp.bfloat16)
    opening = lax.broadcasted_iota(jnp.int32, (rows + lag, 1), 0) < lag
    whole_x = jnp.where(first & opening, jnp.pad(tail_x, ((0, rows), (0, 0))), xzbc[:, :inner])
    whole_bc = jnp.where(first & opening, jnp.pad(tail_bc, ((0, rows), (0, 0))), xzbc[:, 2 * inner :])
    z_val = xzbc[lag:, inner : 2 * inner]
    x_conv = depthwise(whole_x, conv_x)
    bc_conv = depthwise(whole_bc, conv_bc)
    b_val = bc_conv[:, :nstate]
    c_val = bc_conv[:, nstate:]
    logdec = -decay_code.astype(jnp.float32) / (16.0 * rows * seq_count)
    blocks = rows // Q
    xb = x_conv.reshape(blocks, Q, heads, head_dim)
    bb = b_val.reshape(blocks, Q, nstate)
    cb = c_val.reshape(blocks, Q, nstate)
    cum = jnp.cumsum(logdec.reshape(blocks, Q, heads), axis=1)

    tail_decay = jnp.exp(cum[:, -1:, :] - cum)
    decayed_b = (
        jnp.transpose(tail_decay, (0, 2, 1))[..., None] * bb.astype(jnp.float32)[:, None]
    ).astype(jnp.bfloat16)
    added = jnp.einsum("bhsn,bshp->bhpn", decayed_b, xb, preferred_element_type=jnp.float32)
    block_decay = jnp.exp(cum[:, -1, :])
    before = [None]
    running = added[0]
    for b in range(1, blocks):
        before.append(running)
        running = block_decay[b][:, None, None] * running + added[b]
    cum_range = jnp.cumsum(logdec, axis=0)
    range_decay = jnp.exp(cum_range[-1])
    incoming = entering_state(range_decay, running, state_in)

    places = jnp.arange(Q)
    lower = places[:, None] >= places[None, :]
    cumt = jnp.transpose(cum, (0, 2, 1))
    diff = cumt[:, :, :, None] - cumt[:, :, None, :]
    decay = jnp.where(lower, jnp.exp(jnp.where(lower, diff, 0.0)), 0.0)
    scores = jnp.einsum("btn,bsn->bts", cb, bb, preferred_element_type=jnp.float32)
    weights = (decay * scores[:, None]).astype(jnp.bfloat16)
    parts = jnp.einsum("bhts,bshp->bthp", weights, xb, preferred_element_type=jnp.float32)
    pieces_out = [parts[0]]
    for b in range(1, blocks):
        carried = jnp.einsum(
            "tn,hpn->thp", cb[b].astype(jnp.float32), before[b], precision=lax.Precision.HIGHEST
        )
        pieces_out.append(parts[b] + carried * jnp.exp(cum[b])[:, :, None])
    parts = jnp.concatenate(pieces_out, axis=0)

    correction = jnp.einsum(
        "tn,hpn->thp", c_val.astype(jnp.float32), incoming, precision=lax.Precision.HIGHEST
    )
    parts = (parts + correction * jnp.exp(cum_range)[:, :, None]).reshape(rows, inner)
    y_val = parts / nstate + jnp.repeat(skip_gain, head_dim)[None, :] * x_conv.astype(jnp.float32)
    gated = y_val * jax.nn.silu(z_val.astype(jnp.float32))
    scaled = (gated * norm_gain[None, :]).astype(jnp.bfloat16)
    partial_out = lax.dot_general(
        scaled, w_out_cols, (((1,), (1,)), ((), ())), preferred_element_type=jnp.float32
    )
    result = lax.psum_scatter(
        partial_out.astype(jnp.bfloat16), "head", scatter_dimension=1, tiled=True
    ).astype(jnp.float32)
    total_sq = lax.psum(jnp.sum(gated * gated, axis=1), "head")
    meansq = total_sq / (inner * lax.axis_size("head"))
    return (result * lax.rsqrt(meansq[:, None] + 1e-05)).astype(jnp.bfloat16)


def solution(mesh):
    devices = mesh.devices
    majors = [getattr(d, "coords", (0,))[0] for d in devices[:, 0]]
    minor = majors.count(majors[0])
    split = Mesh(devices.reshape(devices.shape[0] // minor, minor, devices.shape[1]), ("sx", "sz", "head"))
    return jax.shard_map(
        local,
        mesh=split,
        in_specs=(
            P(SEQ, None),
            P(SEQ, None, "head"),
            P(SEQ, None),
            P(None, "head"),
            P(),
            P(None, "head"),
            P(),
            P(SEQ, "head"),
            P("head"),
            P("head", None, None),
            P("head"),
            P("head", SEQ),
        ),
        out_specs=P(SEQ, "head"),
        check_vma=False,
    )
```

```python
import functools

import jax
import jax.numpy as jnp
from jax import lax
from jax.experimental import pallas as pl
from jax.experimental.pallas import tpu as pltpu
from jax.sharding import PartitionSpec as P

Q = 256


def passed_along(value, axis, by):
    size = lax.axis_size(axis)
    pairs = [(i, i + by) for i in range(size) if 0 <= i + by < size]
    return lax.ppermute(value, axis, pairs)


def depthwise(whole, kernel):
    whole = whole.astype(jnp.float32)
    length = whole.shape[0] - kernel.shape[0] + 1
    total = jnp.zeros((length, whole.shape[1]), jnp.float32)
    for offset in range(kernel.shape[0]):
        total = total + kernel[offset] * whole[offset : offset + length]
    return jax.nn.silu(total).astype(jnp.bfloat16)


def scan_kernel(count, shifts, msg_ref, dec_ref, sin_ref, out_ref, dec_acc, s_send, a_send, s_recv, a_recv, send_sem, recv_sem):
    me = lax.axis_index("seq")
    hd = lax.axis_index("head")
    barrier = pltpu.get_barrier_semaphore()
    distinct = sorted(set(shifts))
    for d in distinct:
        for peer in ((me + d) % count, (me + count - d) % count):
            pl.semaphore_signal(barrier, inc=1, device_id=(peer, hd), device_id_type=pl.DeviceIdType.MESH)
    pl.semaphore_wait(barrier, 2 * len(distinct))
    copies = []
    for k, d in enumerate(shifts):
        if k == 0:
            s_send[k] = msg_ref[...].astype(s_send.dtype)
            a_send[k] = dec_ref[...]
        else:
            s_send[k] = out_ref[...].astype(s_send.dtype)
            a_send[k] = dec_acc[...]
        target = ((me + d) % count, hd)
        pair = []
        for index, (src, dst) in enumerate(((s_send, s_recv), (a_send, a_recv))):
            copy = pltpu.make_async_remote_copy(
                src_ref=src.at[k],
                dst_ref=dst.at[k],
                send_sem=send_sem.at[index, k],
                recv_sem=recv_sem.at[index, k],
                device_id=target,
                device_id_type=pl.DeviceIdType.MESH,
            )
            copy.start()
            pair.append(copy)
        copies.extend(pair)
        for copy in pair:
            copy.wait_recv()
        far_s = s_recv[k].astype(jnp.float32)
        far_a = a_recv[k]
        if k == 0:
            out_ref[...] = jnp.where(me == 0, sin_ref[...], far_s)
            dec_acc[...] = jnp.where(me == 0, jnp.zeros_like(far_a), far_a)
        else:
            acc_s = out_ref[...]
            acc_a = dec_acc[...]
            rows = acc_s.shape[1]
            acc_a_rows = jnp.tile(acc_a, (1, rows // acc_a.shape[1], 1))
            out_ref[...] = jnp.where(me >= d, acc_a_rows * far_s + acc_s, acc_s)
            dec_acc[...] = jnp.where(me >= d, acc_a * far_a, acc_a)
    for copy in copies:
        copy.wait_send()


def entering_state(decay, end_state, state_in):
    count = lax.axis_size("seq")
    heads, rows, lanes = end_state.shape
    decay_rows = jnp.broadcast_to(decay[:, None, None], (heads, 8, lanes))
    shifts = [1]
    step = 1
    while step < count:
        shifts.append(step)
        step *= 2
    steps = len(shifts)
    return pl.pallas_call(
        functools.partial(scan_kernel, count, tuple(shifts)),
        out_shape=jax.ShapeDtypeStruct(end_state.shape, jnp.float32),
        in_specs=[pl.BlockSpec(memory_space=pltpu.VMEM)] * 3,
        out_specs=pl.BlockSpec(memory_space=pltpu.VMEM),
        scratch_shapes=[
            pltpu.VMEM(decay_rows.shape, jnp.float32),
            pltpu.VMEM((steps,) + end_state.shape, jnp.bfloat16),
            pltpu.VMEM((steps,) + decay_rows.shape, jnp.float32),
            pltpu.VMEM((steps,) + end_state.shape, jnp.bfloat16),
            pltpu.VMEM((steps,) + decay_rows.shape, jnp.float32),
            pltpu.SemaphoreType.DMA((2, steps)),
            pltpu.SemaphoreType.DMA((2, steps)),
        ],
        compiler_params=pltpu.CompilerParams(collective_id=0, has_side_effects=True),
    )(end_state, decay_rows, state_in)


def gather_kernel(count, src_ref, out_ref, own_sem, send_sem, recv_sem):
    me = lax.axis_index("seq")
    hd = lax.axis_index("head")
    rows = src_ref.shape[0]
    barrier = pltpu.get_barrier_semaphore()
    for k in range(1, count):
        pl.semaphore_signal(
            barrier, inc=1, device_id=((me + k) % count, hd), device_id_type=pl.DeviceIdType.MESH
        )
    pl.semaphore_wait(barrier, count - 1)
    place = out_ref.at[pl.ds(me * rows, rows)]
    own = pltpu.make_async_copy(src_ref, place, own_sem)
    own.start()
    copies = []
    for k in range(1, count):
        copy = pltpu.make_async_remote_copy(
            src_ref=src_ref,
            dst_ref=place,
            send_sem=send_sem.at[k],
            recv_sem=recv_sem.at[k],
            device_id=((me + k) % count, hd),
            device_id_type=pl.DeviceIdType.MESH,
        )
        copy.start()
        copies.append(copy)
    for copy in copies:
        copy.wait_recv()
    for copy in copies:
        copy.wait_send()
    own.wait()


def gather_seq(value):
    count = lax.axis_size("seq")
    rows, cols = value.shape
    return pl.pallas_call(
        functools.partial(gather_kernel, count),
        out_shape=jax.ShapeDtypeStruct((count * rows, cols), value.dtype),
        in_specs=[pl.BlockSpec(memory_space=pl.ANY)],
        out_specs=pl.BlockSpec(memory_space=pl.ANY),
        scratch_shapes=[
            pltpu.SemaphoreType.DMA(()),
            pltpu.SemaphoreType.DMA((count,)),
            pltpu.SemaphoreType.DMA((count,)),
        ],
        compiler_params=pltpu.CompilerParams(collective_id=1, has_side_effects=True),
    )(value)


def local(
    tokens,
    w_xz,
    w_bc,
    conv_x,
    conv_bc,
    tail_x,
    tail_bc,
    decay_code,
    skip_gain,
    state_in,
    norm_gain,
    w_out,
):
    rows = tokens.shape[0]
    heads, head_dim, nstate = state_in.shape
    inner = heads * head_dim
    seq_count = lax.axis_size("seq")
    first = lax.axis_index("seq") == 0
    w_x = w_xz[:, 0, :]
    w_z = w_xz[:, 1, :]
    packed = jnp.concatenate([w_x, w_z, w_bc], axis=1)
    gathered = lax.all_gather(packed, "seq", axis=0, tiled=True)
    w_out_cols = gather_seq(jnp.transpose(w_out))
    lag = conv_x.shape[0] - 1
    earlier = passed_along(tokens[rows - lag :], "seq", 1)
    extended = jnp.concatenate([earlier, tokens], axis=0)
    xzbc = jnp.dot(extended, gathered, preferred_element_type=jnp.float32).astype(jnp.bfloat16)
    opening = lax.broadcasted_iota(jnp.int32, (rows + lag, 1), 0) < lag
    whole_x = jnp.where(first & opening, jnp.pad(tail_x, ((0, rows), (0, 0))), xzbc[:, :inner])
    whole_bc = jnp.where(first & opening, jnp.pad(tail_bc, ((0, rows), (0, 0))), xzbc[:, 2 * inner :])
    z_val = xzbc[lag:, inner : 2 * inner]
    x_conv = depthwise(whole_x, conv_x)
    bc_conv = depthwise(whole_bc, conv_bc)
    b_val = bc_conv[:, :nstate]
    c_val = bc_conv[:, nstate:]
    logdec = -decay_code.astype(jnp.float32) / (16.0 * rows * seq_count)
    blocks = rows // Q
    xb = x_conv.reshape(blocks, Q, heads, head_dim)
    bb = b_val.reshape(blocks, Q, nstate)
    cb = c_val.reshape(blocks, Q, nstate)
    cum = jnp.cumsum(logdec.reshape(blocks, Q, heads), axis=1)

    tail_decay = jnp.exp(cum[:, -1:, :] - cum)
    decayed_b = (
        jnp.transpose(tail_decay, (0, 2, 1))[..., None] * bb.astype(jnp.float32)[:, None]
    ).astype(jnp.bfloat16)
    added = jnp.einsum("bhsn,bshp->bhpn", decayed_b, xb, preferred_element_type=jnp.float32)
    block_decay = jnp.exp(cum[:, -1, :])
    before = [None]
    running = added[0]
    for b in range(1, blocks):
        before.append(running)
        running = block_decay[b][:, None, None] * running + added[b]
    cum_range = jnp.cumsum(logdec, axis=0)
    range_decay = jnp.exp(cum_range[-1])
    incoming = entering_state(range_decay, running, state_in)

    places = jnp.arange(Q)
    lower = places[:, None] >= places[None, :]
    cumt = jnp.transpose(cum, (0, 2, 1))
    diff = cumt[:, :, :, None] - cumt[:, :, None, :]
    decay = jnp.where(lower, jnp.exp(jnp.where(lower, diff, 0.0)), 0.0)
    scores = jnp.einsum("btn,bsn->bts", cb, bb, preferred_element_type=jnp.float32)
    weights = (decay * scores[:, None]).astype(jnp.bfloat16)
    parts = jnp.einsum("bhts,bshp->bthp", weights, xb, preferred_element_type=jnp.float32)
    pieces_out = [parts[0]]
    for b in range(1, blocks):
        carried = jnp.einsum(
            "tn,hpn->thp", cb[b].astype(jnp.float32), before[b], precision=lax.Precision.HIGHEST
        )
        pieces_out.append(parts[b] + carried * jnp.exp(cum[b])[:, :, None])
    parts = jnp.concatenate(pieces_out, axis=0)

    correction = jnp.einsum(
        "tn,hpn->thp", c_val.astype(jnp.float32), incoming, precision=lax.Precision.HIGHEST
    )
    parts = (parts + correction * jnp.exp(cum_range)[:, :, None]).reshape(rows, inner)
    y_val = parts / nstate + jnp.repeat(skip_gain, head_dim)[None, :] * x_conv.astype(jnp.float32)
    gated = y_val * jax.nn.silu(z_val.astype(jnp.float32))
    scaled = (gated * norm_gain[None, :]).astype(jnp.bfloat16)
    partial_out = lax.dot_general(
        scaled, w_out_cols, (((1,), (1,)), ((), ())), preferred_element_type=jnp.float32
    )
    result = lax.psum_scatter(
        partial_out.astype(jnp.bfloat16), "head", scatter_dimension=1, tiled=True
    ).astype(jnp.float32)
    total_sq = lax.psum(jnp.sum(gated * gated, axis=1), "head")
    meansq = total_sq / (inner * lax.axis_size("head"))
    return (result * lax.rsqrt(meansq[:, None] + 1e-05)).astype(jnp.bfloat16)


def solution(mesh):
    return jax.shard_map(
        local,
        mesh=mesh,
        in_specs=(
            P("seq", None),
            P("seq", None, "head"),
            P("seq", None),
            P(None, "head"),
            P(),
            P(None, "head"),
            P(),
            P("seq", "head"),
            P("head"),
            P("head", None, None),
            P("head"),
            P("head", "seq"),
        ),
        out_specs=P("seq", "head"),
        check_vma=False,
    )
```

```python
import functools

import jax
import jax.numpy as jnp
from jax import lax
from jax.experimental import pallas as pl
from jax.experimental.pallas import tpu as pltpu
from jax.sharding import PartitionSpec as P

Q = 256


def passed_along(value, axis, by):
    size = lax.axis_size(axis)
    pairs = [(i, i + by) for i in range(size) if 0 <= i + by < size]
    return lax.ppermute(value, axis, pairs)


def depthwise(whole, kernel):
    whole = whole.astype(jnp.float32)
    length = whole.shape[0] - kernel.shape[0] + 1
    total = jnp.zeros((length, whole.shape[1]), jnp.float32)
    for offset in range(kernel.shape[0]):
        total = total + kernel[offset] * whole[offset : offset + length]
    return jax.nn.silu(total).astype(jnp.bfloat16)


def scan_kernel(count, shifts, msg_ref, dec_ref, sin_ref, out_ref, dec_acc, s_send, a_send, s_recv, a_recv, send_sem, recv_sem):
    me = lax.axis_index("seq")
    hd = lax.axis_index("head")
    barrier = pltpu.get_barrier_semaphore()
    distinct = sorted(set(shifts))
    for d in distinct:
        for peer in ((me + d) % count, (me + count - d) % count):
            pl.semaphore_signal(barrier, inc=1, device_id=(peer, hd), device_id_type=pl.DeviceIdType.MESH)
    pl.semaphore_wait(barrier, 2 * len(distinct))
    copies = []
    for k, d in enumerate(shifts):
        if k == 0:
            s_send[k] = msg_ref[...].astype(s_send.dtype)
            a_send[k] = dec_ref[...]
        else:
            s_send[k] = out_ref[...].astype(s_send.dtype)
            a_send[k] = dec_acc[...]
        target = ((me + d) % count, hd)
        pair = []
        for index, (src, dst) in enumerate(((s_send, s_recv), (a_send, a_recv))):
            copy = pltpu.make_async_remote_copy(
                src_ref=src.at[k],
                dst_ref=dst.at[k],
                send_sem=send_sem.at[index, k],
                recv_sem=recv_sem.at[index, k],
                device_id=target,
                device_id_type=pl.DeviceIdType.MESH,
            )
            copy.start()
            pair.append(copy)
        copies.extend(pair)
        for copy in pair:
            copy.wait_recv()
        far_s = s_recv[k].astype(jnp.float32)
        far_a = a_recv[k]
        if k == 0:
            out_ref[...] = jnp.where(me == 0, sin_ref[...], far_s)
            dec_acc[...] = jnp.where(me == 0, jnp.zeros_like(far_a), far_a)
        else:
            acc_s = out_ref[...]
            acc_a = dec_acc[...]
            rows = acc_s.shape[1]
            acc_a_rows = jnp.tile(acc_a, (1, rows // acc_a.shape[1], 1))
            out_ref[...] = jnp.where(me >= d, acc_a_rows * far_s + acc_s, acc_s)
            dec_acc[...] = jnp.where(me >= d, acc_a * far_a, acc_a)
    for copy in copies:
        copy.wait_send()


def entering_state(decay, end_state, state_in):
    count = lax.axis_size("seq")
    heads, rows, lanes = end_state.shape
    decay_rows = jnp.broadcast_to(decay[:, None, None], (heads, 8, lanes))
    shifts = [1]
    step = 1
    while step < count:
        shifts.append(step)
        step *= 2
    steps = len(shifts)
    return pl.pallas_call(
        functools.partial(scan_kernel, count, tuple(shifts)),
        out_shape=jax.ShapeDtypeStruct(end_state.shape, jnp.float32),
        in_specs=[pl.BlockSpec(memory_space=pltpu.VMEM)] * 3,
        out_specs=pl.BlockSpec(memory_space=pltpu.VMEM),
        scratch_shapes=[
            pltpu.VMEM(decay_rows.shape, jnp.float32),
            pltpu.VMEM((steps,) + end_state.shape, jnp.bfloat16),
            pltpu.VMEM((steps,) + decay_rows.shape, jnp.float32),
            pltpu.VMEM((steps,) + end_state.shape, jnp.bfloat16),
            pltpu.VMEM((steps,) + decay_rows.shape, jnp.float32),
            pltpu.SemaphoreType.DMA((2, steps)),
            pltpu.SemaphoreType.DMA((2, steps)),
        ],
        compiler_params=pltpu.CompilerParams(collective_id=0, has_side_effects=True),
    )(end_state, decay_rows, state_in)


def ring_kernel(count, src_ref, out_ref, own_sem, send_r, recv_r, send_l, recv_l):
    me = lax.axis_index("seq")
    hd = lax.axis_index("head")
    rows = src_ref.shape[0]
    right = (me + 1) % count
    left = (me + count - 1) % count
    barrier = pltpu.get_barrier_semaphore()
    for peer in (left, right):
        pl.semaphore_signal(barrier, inc=1, device_id=(peer, hd), device_id_type=pl.DeviceIdType.MESH)
    pl.semaphore_wait(barrier, 2)
    own = pltpu.make_async_copy(src_ref, out_ref.at[pl.ds(me * rows, rows)], own_sem)
    own.start()
    to_right = count // 2
    to_left = count - 1 - to_right
    copies = []
    for t in range(max(to_right, to_left)):
        step = []
        for steps, sign, peer, sends, recvs in ((to_right, -1, right, send_r, recv_r), (to_left, 1, left, send_l, recv_l)):
            if t >= steps:
                continue
            block = (me + sign * t + count) % count
            place = out_ref.at[pl.ds(block * rows, rows)]
            copy = pltpu.make_async_remote_copy(
                src_ref=src_ref if t == 0 else place,
                dst_ref=place,
                send_sem=sends.at[t],
                recv_sem=recvs.at[t],
                device_id=(peer, hd),
                device_id_type=pl.DeviceIdType.MESH,
            )
            copy.start()
            step.append(copy)
        for copy in step:
            copy.wait_recv()
        copies.extend(step)
    for copy in copies:
        copy.wait_send()
    own.wait()


def gather_seq(value):
    count = lax.axis_size("seq")
    rows, cols = value.shape
    to_right = count // 2
    to_left = count - 1 - to_right
    return pl.pallas_call(
        functools.partial(ring_kernel, count),
        out_shape=jax.ShapeDtypeStruct((count * rows, cols), value.dtype),
        in_specs=[pl.BlockSpec(memory_space=pl.ANY)],
        out_specs=pl.BlockSpec(memory_space=pl.ANY),
        scratch_shapes=[
            pltpu.SemaphoreType.DMA(()),
            pltpu.SemaphoreType.DMA((to_right,)),
            pltpu.SemaphoreType.DMA((to_right,)),
            pltpu.SemaphoreType.DMA((max(to_left, 1),)),
            pltpu.SemaphoreType.DMA((max(to_left, 1),)),
        ],
        compiler_params=pltpu.CompilerParams(collective_id=1, has_side_effects=True),
    )(value)


def local(
    tokens,
    w_xz,
    w_bc,
    conv_x,
    conv_bc,
    tail_x,
    tail_bc,
    decay_code,
    skip_gain,
    state_in,
    norm_gain,
    w_out,
):
    rows = tokens.shape[0]
    heads, head_dim, nstate = state_in.shape
    inner = heads * head_dim
    seq_count = lax.axis_size("seq")
    first = lax.axis_index("seq") == 0
    w_x = w_xz[:, 0, :]
    w_z = w_xz[:, 1, :]
    packed = jnp.concatenate([w_x, w_z, w_bc], axis=1)
    gathered = lax.all_gather(packed, "seq", axis=0, tiled=True)
    w_out_cols = gather_seq(jnp.transpose(w_out))
    lag = conv_x.shape[0] - 1
    earlier = passed_along(tokens[rows - lag :], "seq", 1)
    extended = jnp.concatenate([earlier, tokens], axis=0)
    xzbc = jnp.dot(extended, gathered, preferred_element_type=jnp.float32).astype(jnp.bfloat16)
    opening = lax.broadcasted_iota(jnp.int32, (rows + lag, 1), 0) < lag
    whole_x = jnp.where(first & opening, jnp.pad(tail_x, ((0, rows), (0, 0))), xzbc[:, :inner])
    whole_bc = jnp.where(first & opening, jnp.pad(tail_bc, ((0, rows), (0, 0))), xzbc[:, 2 * inner :])
    z_val = xzbc[lag:, inner : 2 * inner]
    x_conv = depthwise(whole_x, conv_x)
    bc_conv = depthwise(whole_bc, conv_bc)
    b_val = bc_conv[:, :nstate]
    c_val = bc_conv[:, nstate:]
    logdec = -decay_code.astype(jnp.float32) / (16.0 * rows * seq_count)
    blocks = rows // Q
    xb = x_conv.reshape(blocks, Q, heads, head_dim)
    bb = b_val.reshape(blocks, Q, nstate)
    cb = c_val.reshape(blocks, Q, nstate)
    cum = jnp.cumsum(logdec.reshape(blocks, Q, heads), axis=1)

    tail_decay = jnp.exp(cum[:, -1:, :] - cum)
    decayed_b = (
        jnp.transpose(tail_decay, (0, 2, 1))[..., None] * bb.astype(jnp.float32)[:, None]
    ).astype(jnp.bfloat16)
    added = jnp.einsum("bhsn,bshp->bhpn", decayed_b, xb, preferred_element_type=jnp.float32)
    block_decay = jnp.exp(cum[:, -1, :])
    before = [None]
    running = added[0]
    for b in range(1, blocks):
        before.append(running)
        running = block_decay[b][:, None, None] * running + added[b]
    cum_range = jnp.cumsum(logdec, axis=0)
    range_decay = jnp.exp(cum_range[-1])
    incoming = entering_state(range_decay, running, state_in)

    places = jnp.arange(Q)
    lower = places[:, None] >= places[None, :]
    cumt = jnp.transpose(cum, (0, 2, 1))
    diff = cumt[:, :, :, None] - cumt[:, :, None, :]
    decay = jnp.where(lower, jnp.exp(jnp.where(lower, diff, 0.0)), 0.0)
    scores = jnp.einsum("btn,bsn->bts", cb, bb, preferred_element_type=jnp.float32)
    weights = (decay * scores[:, None]).astype(jnp.bfloat16)
    parts = jnp.einsum("bhts,bshp->bthp", weights, xb, preferred_element_type=jnp.float32)
    pieces_out = [parts[0]]
    for b in range(1, blocks):
        carried = jnp.einsum(
            "tn,hpn->thp", cb[b].astype(jnp.float32), before[b], precision=lax.Precision.HIGHEST
        )
        pieces_out.append(parts[b] + carried * jnp.exp(cum[b])[:, :, None])
    parts = jnp.concatenate(pieces_out, axis=0)

    correction = jnp.einsum(
        "tn,hpn->thp", c_val.astype(jnp.float32), incoming, precision=lax.Precision.HIGHEST
    )
    parts = (parts + correction * jnp.exp(cum_range)[:, :, None]).reshape(rows, inner)
    y_val = parts / nstate + jnp.repeat(skip_gain, head_dim)[None, :] * x_conv.astype(jnp.float32)
    gated = y_val * jax.nn.silu(z_val.astype(jnp.float32))
    scaled = (gated * norm_gain[None, :]).astype(jnp.bfloat16)
    partial_out = lax.dot_general(
        scaled, w_out_cols, (((1,), (1,)), ((), ())), preferred_element_type=jnp.float32
    )
    result = lax.psum_scatter(
        partial_out.astype(jnp.bfloat16), "head", scatter_dimension=1, tiled=True
    ).astype(jnp.float32)
    total_sq = lax.psum(jnp.sum(gated * gated, axis=1), "head")
    meansq = total_sq / (inner * lax.axis_size("head"))
    return (result * lax.rsqrt(meansq[:, None] + 1e-05)).astype(jnp.bfloat16)


def solution(mesh):
    return jax.shard_map(
        local,
        mesh=mesh,
        in_specs=(
            P("seq", None),
            P("seq", None, "head"),
            P("seq", None),
            P(None, "head"),
            P(),
            P(None, "head"),
            P(),
            P("seq", "head"),
            P("head"),
            P("head", None, None),
            P("head"),
            P("head", "seq"),
        ),
        out_specs=P("seq", "head"),
        check_vma=False,
    )
```

```python
import functools

import jax
import jax.numpy as jnp
from jax import lax
from jax.experimental import pallas as pl
from jax.experimental.pallas import tpu as pltpu
from jax.sharding import PartitionSpec as P

Q = 256


def passed_along(value, axis, by):
    size = lax.axis_size(axis)
    pairs = [(i, i + by) for i in range(size) if 0 <= i + by < size]
    return lax.ppermute(value, axis, pairs)


def depthwise(whole, kernel):
    whole = whole.astype(jnp.float32)
    length = whole.shape[0] - kernel.shape[0] + 1
    total = jnp.zeros((length, whole.shape[1]), jnp.float32)
    for offset in range(kernel.shape[0]):
        total = total + kernel[offset] * whole[offset : offset + length]
    return jax.nn.silu(total).astype(jnp.bfloat16)


def scan_kernel(count, shifts, msg_ref, dec_ref, sin_ref, out_ref, dec_acc, s_send, a_send, s_recv, a_recv, send_sem, recv_sem):
    me = lax.axis_index("seq")
    hd = lax.axis_index("head")
    barrier = pltpu.get_barrier_semaphore()
    distinct = sorted(set(shifts))
    for d in distinct:
        for peer in ((me + d) % count, (me + count - d) % count):
            pl.semaphore_signal(barrier, inc=1, device_id=(peer, hd), device_id_type=pl.DeviceIdType.MESH)
    pl.semaphore_wait(barrier, 2 * len(distinct))
    copies = []
    for k, d in enumerate(shifts):
        if k == 0:
            s_send[k] = msg_ref[...].astype(s_send.dtype)
            a_send[k] = dec_ref[...]
        else:
            s_send[k] = out_ref[...].astype(s_send.dtype)
            a_send[k] = dec_acc[...]
        target = ((me + d) % count, hd)
        pair = []
        for index, (src, dst) in enumerate(((s_send, s_recv), (a_send, a_recv))):
            copy = pltpu.make_async_remote_copy(
                src_ref=src.at[k],
                dst_ref=dst.at[k],
                send_sem=send_sem.at[index, k],
                recv_sem=recv_sem.at[index, k],
                device_id=target,
                device_id_type=pl.DeviceIdType.MESH,
            )
            copy.start()
            pair.append(copy)
        copies.extend(pair)
        for copy in pair:
            copy.wait_recv()
        far_s = s_recv[k].astype(jnp.float32)
        far_a = a_recv[k]
        if k == 0:
            out_ref[...] = jnp.where(me == 0, sin_ref[...], far_s)
            dec_acc[...] = jnp.where(me == 0, jnp.zeros_like(far_a), far_a)
        else:
            acc_s = out_ref[...]
            acc_a = dec_acc[...]
            rows = acc_s.shape[1]
            acc_a_rows = jnp.tile(acc_a, (1, rows // acc_a.shape[1], 1))
            out_ref[...] = jnp.where(me >= d, acc_a_rows * far_s + acc_s, acc_s)
            dec_acc[...] = jnp.where(me >= d, acc_a * far_a, acc_a)
    for copy in copies:
        copy.wait_send()


def entering_state(decay, end_state, state_in):
    count = lax.axis_size("seq")
    heads, rows, lanes = end_state.shape
    decay_rows = jnp.broadcast_to(decay[:, None, None], (heads, 8, lanes))
    shifts = [1]
    step = 1
    while step < count:
        shifts.append(step)
        step *= 2
    steps = len(shifts)
    return pl.pallas_call(
        functools.partial(scan_kernel, count, tuple(shifts)),
        out_shape=jax.ShapeDtypeStruct(end_state.shape, jnp.float32),
        in_specs=[pl.BlockSpec(memory_space=pltpu.VMEM)] * 3,
        out_specs=pl.BlockSpec(memory_space=pltpu.VMEM),
        scratch_shapes=[
            pltpu.VMEM(decay_rows.shape, jnp.float32),
            pltpu.VMEM((steps,) + end_state.shape, jnp.bfloat16),
            pltpu.VMEM((steps,) + decay_rows.shape, jnp.float32),
            pltpu.VMEM((steps,) + end_state.shape, jnp.bfloat16),
            pltpu.VMEM((steps,) + decay_rows.shape, jnp.float32),
            pltpu.SemaphoreType.DMA((2, steps)),
            pltpu.SemaphoreType.DMA((2, steps)),
        ],
        compiler_params=pltpu.CompilerParams(collective_id=0, has_side_effects=True),
    )(end_state, decay_rows, state_in)


def local(
    tokens,
    w_xz,
    w_bc,
    conv_x,
    conv_bc,
    tail_x,
    tail_bc,
    decay_code,
    skip_gain,
    state_in,
    norm_gain,
    w_out,
):
    rows = tokens.shape[0]
    heads, head_dim, nstate = state_in.shape
    inner = heads * head_dim
    seq_count = lax.axis_size("seq")
    first = lax.axis_index("seq") == 0
    w_x = w_xz[:, 0, :]
    w_z = w_xz[:, 1, :]
    packed = jnp.concatenate([w_x, w_z, w_bc], axis=1)
    gathered = lax.all_gather(packed, "seq", axis=0, tiled=True)
    w_out_cols = lax.all_gather(jnp.transpose(w_out), "seq", axis=0, tiled=True)
    lag = conv_x.shape[0] - 1
    earlier = passed_along(tokens[rows - lag :], "seq", 1)
    extended = jnp.concatenate([earlier, tokens], axis=0)
    xzbc = jnp.dot(extended, gathered, preferred_element_type=jnp.float32).astype(jnp.bfloat16)
    opening = lax.broadcasted_iota(jnp.int32, (rows + lag, 1), 0) < lag
    whole_x = jnp.where(first & opening, jnp.pad(tail_x, ((0, rows), (0, 0))), xzbc[:, :inner])
    whole_bc = jnp.where(first & opening, jnp.pad(tail_bc, ((0, rows), (0, 0))), xzbc[:, 2 * inner :])
    z_val = xzbc[lag:, inner : 2 * inner]
    x_conv = depthwise(whole_x, conv_x)
    bc_conv = depthwise(whole_bc, conv_bc)
    b_val = bc_conv[:, :nstate]
    c_val = bc_conv[:, nstate:]
    logdec = -decay_code.astype(jnp.float32) / (16.0 * rows * seq_count)
    blocks = rows // Q
    xb = x_conv.reshape(blocks, Q, heads, head_dim)
    bb = b_val.reshape(blocks, Q, nstate)
    cb = c_val.reshape(blocks, Q, nstate)
    cum = jnp.cumsum(logdec.reshape(blocks, Q, heads), axis=1)

    tail_decay = jnp.exp(cum[:, -1:, :] - cum)
    decayed_b = (
        jnp.transpose(tail_decay, (0, 2, 1))[..., None] * bb.astype(jnp.float32)[:, None]
    ).astype(jnp.bfloat16)
    added = jnp.einsum("bhsn,bshp->bhpn", decayed_b, xb, preferred_element_type=jnp.float32)
    block_decay = jnp.exp(cum[:, -1, :])
    before = [None]
    running = added[0]
    for b in range(1, blocks):
        before.append(running)
        running = block_decay[b][:, None, None] * running + added[b]
    cum_range = jnp.cumsum(logdec, axis=0)
    range_decay = jnp.exp(cum_range[-1])
    incoming = entering_state(range_decay, running, state_in)

    places = jnp.arange(Q)
    lower = places[:, None] >= places[None, :]
    cumt = jnp.transpose(cum, (0, 2, 1))
    diff = cumt[:, :, :, None] - cumt[:, :, None, :]
    decay = jnp.where(lower, jnp.exp(jnp.where(lower, diff, 0.0)), 0.0)
    scores = jnp.einsum("btn,bsn->bts", cb, bb, preferred_element_type=jnp.float32)
    weights = (decay * scores[:, None]).astype(jnp.bfloat16)
    parts = jnp.einsum("bhts,bshp->bthp", weights, xb, preferred_element_type=jnp.float32)
    pieces_out = [parts[0]]
    for b in range(1, blocks):
        carried = jnp.einsum(
            "tn,hpn->thp", cb[b].astype(jnp.float32), before[b], precision=lax.Precision.HIGHEST
        )
        pieces_out.append(parts[b] + carried * jnp.exp(cum[b])[:, :, None])
    parts = jnp.concatenate(pieces_out, axis=0)

    correction = jnp.einsum(
        "tn,hpn->thp", c_val.astype(jnp.float32), incoming, precision=lax.Precision.HIGHEST
    )
    parts = (parts + correction * jnp.exp(cum_range)[:, :, None]).reshape(rows, inner)
    y_val = parts / nstate + jnp.repeat(skip_gain, head_dim)[None, :] * x_conv.astype(jnp.float32)
    gated = y_val * jax.nn.silu(z_val.astype(jnp.float32))
    scaled = (gated * norm_gain[None, :]).astype(jnp.bfloat16)
    partial_t = lax.dot_general(
        w_out_cols, scaled, (((1,), (1,)), ((), ())), preferred_element_type=jnp.float32
    )
    result = jnp.transpose(
        lax.psum_scatter(partial_t.astype(jnp.bfloat16), "head", scatter_dimension=0, tiled=True)
    ).astype(jnp.float32)
    total_sq = lax.psum(jnp.sum(gated * gated, axis=1), "head")
    meansq = total_sq / (inner * lax.axis_size("head"))
    return (result * lax.rsqrt(meansq[:, None] + 1e-05)).astype(jnp.bfloat16)


def solution(mesh):
    return jax.shard_map(
        local,
        mesh=mesh,
        in_specs=(
            P("seq", None),
            P("seq", None, "head"),
            P("seq", None),
            P(None, "head"),
            P(),
            P(None, "head"),
            P(),
            P("seq", "head"),
            P("head"),
            P("head", None, None),
            P("head"),
            P("head", "seq"),
        ),
        out_specs=P("seq", "head"),
        check_vma=False,
    )
```

```python
import functools

import jax
import jax.numpy as jnp
from jax import lax
from jax.experimental import pallas as pl
from jax.experimental.pallas import tpu as pltpu
from jax.sharding import Mesh, PartitionSpec as P

Q = 256


HEAD = ("hy", "hc")


def head_size():
    return lax.axis_size("hy") * lax.axis_size("hc")


def passed_along(value, axis, by):
    size = lax.axis_size(axis)
    pairs = [(i, i + by) for i in range(size) if 0 <= i + by < size]
    return lax.ppermute(value, axis, pairs)


def depthwise(whole, kernel):
    whole = whole.astype(jnp.float32)
    length = whole.shape[0] - kernel.shape[0] + 1
    total = jnp.zeros((length, whole.shape[1]), jnp.float32)
    for offset in range(kernel.shape[0]):
        total = total + kernel[offset] * whole[offset : offset + length]
    return jax.nn.silu(total).astype(jnp.bfloat16)


def scan_kernel(count, shifts, msg_ref, dec_ref, sin_ref, out_ref, dec_acc, s_send, a_send, s_recv, a_recv, send_sem, recv_sem):
    me = lax.axis_index("seq")
    hy = lax.axis_index("hy")
    hc = lax.axis_index("hc")
    barrier = pltpu.get_barrier_semaphore()
    distinct = sorted(set(shifts))
    for d in distinct:
        for peer in ((me + d) % count, (me + count - d) % count):
            pl.semaphore_signal(barrier, inc=1, device_id=(peer, hy, hc), device_id_type=pl.DeviceIdType.MESH)
    pl.semaphore_wait(barrier, 2 * len(distinct))
    copies = []
    for k, d in enumerate(shifts):
        if k == 0:
            s_send[k] = msg_ref[...].astype(s_send.dtype)
            a_send[k] = dec_ref[...]
        else:
            s_send[k] = out_ref[...].astype(s_send.dtype)
            a_send[k] = dec_acc[...]
        target = ((me + d) % count, hy, hc)
        pair = []
        for index, (src, dst) in enumerate(((s_send, s_recv), (a_send, a_recv))):
            copy = pltpu.make_async_remote_copy(
                src_ref=src.at[k],
                dst_ref=dst.at[k],
                send_sem=send_sem.at[index, k],
                recv_sem=recv_sem.at[index, k],
                device_id=target,
                device_id_type=pl.DeviceIdType.MESH,
            )
            copy.start()
            pair.append(copy)
        copies.extend(pair)
        for copy in pair:
            copy.wait_recv()
        far_s = s_recv[k].astype(jnp.float32)
        far_a = a_recv[k]
        if k == 0:
            out_ref[...] = jnp.where(me == 0, sin_ref[...], far_s)
            dec_acc[...] = jnp.where(me == 0, jnp.zeros_like(far_a), far_a)
        else:
            acc_s = out_ref[...]
            acc_a = dec_acc[...]
            rows = acc_s.shape[1]
            acc_a_rows = jnp.tile(acc_a, (1, rows // acc_a.shape[1], 1))
            out_ref[...] = jnp.where(me >= d, acc_a_rows * far_s + acc_s, acc_s)
            dec_acc[...] = jnp.where(me >= d, acc_a * far_a, acc_a)
    for copy in copies:
        copy.wait_send()


def entering_state(decay, end_state, state_in):
    count = lax.axis_size("seq")
    heads, rows, lanes = end_state.shape
    decay_rows = jnp.broadcast_to(decay[:, None, None], (heads, 8, lanes))
    shifts = [1]
    step = 1
    while step < count:
        shifts.append(step)
        step *= 2
    steps = len(shifts)
    return pl.pallas_call(
        functools.partial(scan_kernel, count, tuple(shifts)),
        out_shape=jax.ShapeDtypeStruct(end_state.shape, jnp.float32),
        in_specs=[pl.BlockSpec(memory_space=pltpu.VMEM)] * 3,
        out_specs=pl.BlockSpec(memory_space=pltpu.VMEM),
        scratch_shapes=[
            pltpu.VMEM(decay_rows.shape, jnp.float32),
            pltpu.VMEM((steps,) + end_state.shape, jnp.bfloat16),
            pltpu.VMEM((steps,) + decay_rows.shape, jnp.float32),
            pltpu.VMEM((steps,) + end_state.shape, jnp.bfloat16),
            pltpu.VMEM((steps,) + decay_rows.shape, jnp.float32),
            pltpu.SemaphoreType.DMA((2, steps)),
            pltpu.SemaphoreType.DMA((2, steps)),
        ],
        compiler_params=pltpu.CompilerParams(collective_id=0, has_side_effects=True),
    )(end_state, decay_rows, state_in)


def local(
    tokens,
    w_xz,
    w_bc,
    conv_x,
    conv_bc,
    tail_x,
    tail_bc,
    decay_code,
    skip_gain,
    state_in,
    norm_gain,
    w_out,
):
    rows = tokens.shape[0]
    heads, head_dim, nstate = state_in.shape
    inner = heads * head_dim
    seq_count = lax.axis_size("seq")
    first = lax.axis_index("seq") == 0
    w_x = w_xz[:, 0, :]
    w_z = w_xz[:, 1, :]
    packed = jnp.concatenate([w_x, w_z, w_bc], axis=1)
    gathered = lax.all_gather(packed, "seq", axis=0, tiled=True)
    w_out_cols = lax.all_gather(jnp.transpose(w_out), "seq", axis=0, tiled=True)
    lag = conv_x.shape[0] - 1
    earlier = passed_along(tokens[rows - lag :], "seq", 1)
    extended = jnp.concatenate([earlier, tokens], axis=0)
    xzbc = jnp.dot(extended, gathered, preferred_element_type=jnp.float32).astype(jnp.bfloat16)
    opening = lax.broadcasted_iota(jnp.int32, (rows + lag, 1), 0) < lag
    whole_x = jnp.where(first & opening, jnp.pad(tail_x, ((0, rows), (0, 0))), xzbc[:, :inner])
    whole_bc = jnp.where(first & opening, jnp.pad(tail_bc, ((0, rows), (0, 0))), xzbc[:, 2 * inner :])
    z_val = xzbc[lag:, inner : 2 * inner]
    x_conv = depthwise(whole_x, conv_x)
    bc_conv = depthwise(whole_bc, conv_bc)
    b_val = bc_conv[:, :nstate]
    c_val = bc_conv[:, nstate:]
    logdec = -decay_code.astype(jnp.float32) / (16.0 * rows * seq_count)
    blocks = rows // Q
    xb = x_conv.reshape(blocks, Q, heads, head_dim)
    bb = b_val.reshape(blocks, Q, nstate)
    cb = c_val.reshape(blocks, Q, nstate)
    cum = jnp.cumsum(logdec.reshape(blocks, Q, heads), axis=1)

    tail_decay = jnp.exp(cum[:, -1:, :] - cum)
    decayed_b = (
        jnp.transpose(tail_decay, (0, 2, 1))[..., None] * bb.astype(jnp.float32)[:, None]
    ).astype(jnp.bfloat16)
    added = jnp.einsum("bhsn,bshp->bhpn", decayed_b, xb, preferred_element_type=jnp.float32)
    block_decay = jnp.exp(cum[:, -1, :])
    before = [None]
    running = added[0]
    for b in range(1, blocks):
        before.append(running)
        running = block_decay[b][:, None, None] * running + added[b]
    cum_range = jnp.cumsum(logdec, axis=0)
    range_decay = jnp.exp(cum_range[-1])
    incoming = entering_state(range_decay, running, state_in)

    places = jnp.arange(Q)
    lower = places[:, None] >= places[None, :]
    cumt = jnp.transpose(cum, (0, 2, 1))
    diff = cumt[:, :, :, None] - cumt[:, :, None, :]
    decay = jnp.where(lower, jnp.exp(jnp.where(lower, diff, 0.0)), 0.0)
    scores = jnp.einsum("btn,bsn->bts", cb, bb, preferred_element_type=jnp.float32)
    weights = (decay * scores[:, None]).astype(jnp.bfloat16)
    parts = jnp.einsum("bhts,bshp->bthp", weights, xb, preferred_element_type=jnp.float32)
    pieces_out = [parts[0]]
    for b in range(1, blocks):
        carried = jnp.einsum(
            "tn,hpn->thp", cb[b].astype(jnp.float32), before[b], precision=lax.Precision.HIGHEST
        )
        pieces_out.append(parts[b] + carried * jnp.exp(cum[b])[:, :, None])
    parts = jnp.concatenate(pieces_out, axis=0)

    correction = jnp.einsum(
        "tn,hpn->thp", c_val.astype(jnp.float32), incoming, precision=lax.Precision.HIGHEST
    )
    parts = (parts + correction * jnp.exp(cum_range)[:, :, None]).reshape(rows, inner)
    y_val = parts / nstate + jnp.repeat(skip_gain, head_dim)[None, :] * x_conv.astype(jnp.float32)
    gated = y_val * jax.nn.silu(z_val.astype(jnp.float32))
    scaled = (gated * norm_gain[None, :]).astype(jnp.bfloat16)
    partial_t = lax.dot_general(
        w_out_cols, scaled, (((1,), (1,)), ((), ())), preferred_element_type=jnp.float32
    )
    cores = lax.axis_size("hc")
    mine = lax.axis_index("hc")
    split = partial_t.reshape(lax.axis_size("hy"), cores, -1, partial_t.shape[1])
    other = jnp.where(mine == 0, split[:, 1], split[:, 0])
    kept = jnp.where(mine == 0, split[:, 0], split[:, 1])
    got = lax.ppermute(other.astype(jnp.bfloat16), "hc", [(i, (i + 1) % cores) for i in range(cores)])
    chip_sum = (kept + got.astype(jnp.float32)).astype(jnp.bfloat16)
    result = jnp.transpose(
        lax.psum_scatter(chip_sum, "hy", scatter_dimension=0, tiled=False)
    ).astype(jnp.float32)
    total_sq = lax.psum(jnp.sum(gated * gated, axis=1), HEAD)
    meansq = total_sq / (inner * head_size())
    return (result * lax.rsqrt(meansq[:, None] + 1e-05)).astype(jnp.bfloat16)


def solution(mesh):
    devices = mesh.devices
    cores = 2 if devices.shape[1] % 2 == 0 else 1
    split = Mesh(devices.reshape(devices.shape[0], devices.shape[1] // cores, cores), ("seq", "hy", "hc"))
    return jax.shard_map(
        local,
        mesh=split,
        in_specs=(
            P("seq", None),
            P("seq", None, HEAD),
            P("seq", None),
            P(None, HEAD),
            P(),
            P(None, HEAD),
            P(),
            P("seq", HEAD),
            P(HEAD),
            P(HEAD, None, None),
            P(HEAD),
            P(HEAD, "seq"),
        ),
        out_specs=P("seq", HEAD),
        check_vma=False,
    )
```

```python
import functools

import jax
import jax.numpy as jnp
from jax import lax
from jax.experimental import pallas as pl
from jax.experimental.pallas import tpu as pltpu
from jax.sharding import PartitionSpec as P

Q = 256


def passed_along(value, axis, by):
    size = lax.axis_size(axis)
    pairs = [(i, i + by) for i in range(size) if 0 <= i + by < size]
    return lax.ppermute(value, axis, pairs)


def depthwise(whole, kernel):
    whole = whole.astype(jnp.float32)
    length = whole.shape[0] - kernel.shape[0] + 1
    total = jnp.zeros((length, whole.shape[1]), jnp.float32)
    for offset in range(kernel.shape[0]):
        total = total + kernel[offset] * whole[offset : offset + length]
    return jax.nn.silu(total).astype(jnp.bfloat16)


def scan_kernel(count, shifts, msg_ref, dec_ref, sin_ref, out_ref, dec_acc, s_send, a_send, s_recv, a_recv, send_sem, recv_sem):
    me = lax.axis_index("seq")
    hd = lax.axis_index("head")
    barrier = pltpu.get_barrier_semaphore()
    distinct = sorted(set(shifts))
    for d in distinct:
        for peer in ((me + d) % count, (me + count - d) % count):
            pl.semaphore_signal(barrier, inc=1, device_id=(peer, hd), device_id_type=pl.DeviceIdType.MESH)
    pl.semaphore_wait(barrier, 2 * len(distinct))
    copies = []
    for k, d in enumerate(shifts):
        if k == 0:
            s_send[k] = msg_ref[...].astype(s_send.dtype)
            a_send[k] = dec_ref[...]
        else:
            s_send[k] = out_ref[...].astype(s_send.dtype)
            a_send[k] = dec_acc[...]
        target = ((me + d) % count, hd)
        pair = []
        for index, (src, dst) in enumerate(((s_send, s_recv), (a_send, a_recv))):
            copy = pltpu.make_async_remote_copy(
                src_ref=src.at[k],
                dst_ref=dst.at[k],
                send_sem=send_sem.at[index, k],
                recv_sem=recv_sem.at[index, k],
                device_id=target,
                device_id_type=pl.DeviceIdType.MESH,
            )
            copy.start()
            pair.append(copy)
        copies.extend(pair)
        for copy in pair:
            copy.wait_recv()
        far_s = s_recv[k].astype(jnp.float32)
        far_a = a_recv[k]
        if k == 0:
            out_ref[...] = jnp.where(me == 0, sin_ref[...], far_s)
            dec_acc[...] = jnp.where(me == 0, jnp.zeros_like(far_a), far_a)
        else:
            acc_s = out_ref[...]
            acc_a = dec_acc[...]
            out_ref[...] = jnp.where(me >= d, acc_a[:, None, :] * far_s + acc_s, acc_s)
            dec_acc[...] = jnp.where(me >= d, acc_a * far_a, acc_a)
    for copy in copies:
        copy.wait_send()


def entering_state(decay, end_state, state_in):
    count = lax.axis_size("seq")
    heads, rows, lanes = end_state.shape
    decay_rows = jnp.broadcast_to(decay[:, None], (heads, lanes))
    shifts = [1]
    step = 1
    while step < count:
        shifts.append(step)
        step *= 2
    steps = len(shifts)
    return pl.pallas_call(
        functools.partial(scan_kernel, count, tuple(shifts)),
        out_shape=jax.ShapeDtypeStruct(end_state.shape, jnp.float32),
        in_specs=[pl.BlockSpec(memory_space=pltpu.VMEM)] * 3,
        out_specs=pl.BlockSpec(memory_space=pltpu.VMEM),
        scratch_shapes=[
            pltpu.VMEM(decay_rows.shape, jnp.float32),
            pltpu.VMEM((steps,) + end_state.shape, jnp.bfloat16),
            pltpu.VMEM((steps,) + decay_rows.shape, jnp.float32),
            pltpu.VMEM((steps,) + end_state.shape, jnp.bfloat16),
            pltpu.VMEM((steps,) + decay_rows.shape, jnp.float32),
            pltpu.SemaphoreType.DMA((2, steps)),
            pltpu.SemaphoreType.DMA((2, steps)),
        ],
        compiler_params=pltpu.CompilerParams(collective_id=0, has_side_effects=True),
    )(end_state, decay_rows, state_in)


def local(
    tokens,
    w_xz,
    w_bc,
    conv_x,
    conv_bc,
    tail_x,
    tail_bc,
    decay_code,
    skip_gain,
    state_in,
    norm_gain,
    w_out,
):
    rows = tokens.shape[0]
    heads, head_dim, nstate = state_in.shape
    inner = heads * head_dim
    seq_count = lax.axis_size("seq")
    first = lax.axis_index("seq") == 0
    w_x = w_xz[:, 0, :]
    w_z = w_xz[:, 1, :]
    packed = jnp.concatenate([w_x, w_z, w_bc], axis=1)
    gathered = lax.all_gather(packed, "seq", axis=0, tiled=True)
    w_out_cols = lax.all_gather(jnp.transpose(w_out), "seq", axis=0, tiled=True)
    lag = conv_x.shape[0] - 1
    earlier = passed_along(tokens[rows - lag :], "seq", 1)
    extended = jnp.concatenate([earlier, tokens], axis=0)
    xzbc = jnp.dot(extended, gathered, preferred_element_type=jnp.float32).astype(jnp.bfloat16)
    opening = lax.broadcasted_iota(jnp.int32, (rows + lag, 1), 0) < lag
    whole_x = jnp.where(first & opening, jnp.pad(tail_x, ((0, rows), (0, 0))), xzbc[:, :inner])
    whole_bc = jnp.where(first & opening, jnp.pad(tail_bc, ((0, rows), (0, 0))), xzbc[:, 2 * inner :])
    z_val = xzbc[lag:, inner : 2 * inner]
    x_conv = depthwise(whole_x, conv_x)
    bc_conv = depthwise(whole_bc, conv_bc)
    b_val = bc_conv[:, :nstate]
    c_val = bc_conv[:, nstate:]
    logdec = -decay_code.astype(jnp.float32) / (16.0 * rows * seq_count)
    blocks = rows // Q
    xb = x_conv.reshape(blocks, Q, heads, head_dim)
    bb = b_val.reshape(blocks, Q, nstate)
    cb = c_val.reshape(blocks, Q, nstate)
    cum = jnp.cumsum(logdec.reshape(blocks, Q, heads), axis=1)

    tail_decay = jnp.exp(cum[:, -1:, :] - cum)
    decayed_b = (
        jnp.transpose(tail_decay, (0, 2, 1))[..., None] * bb.astype(jnp.float32)[:, None]
    ).astype(jnp.bfloat16)
    added = jnp.einsum("bhsn,bshp->bhpn", decayed_b, xb, preferred_element_type=jnp.float32)
    block_decay = jnp.exp(cum[:, -1, :])
    before = [None]
    running = added[0]
    for b in range(1, blocks):
        before.append(running)
        running = block_decay[b][:, None, None] * running + added[b]
    cum_range = jnp.cumsum(logdec, axis=0)
    range_decay = jnp.exp(cum_range[-1])
    incoming = entering_state(range_decay, running, state_in)

    places = jnp.arange(Q)
    lower = places[:, None] >= places[None, :]
    cumt = jnp.transpose(cum, (0, 2, 1))
    diff = cumt[:, :, :, None] - cumt[:, :, None, :]
    decay = jnp.where(lower, jnp.exp(jnp.where(lower, diff, 0.0)), 0.0)
    scores = jnp.einsum("btn,bsn->bts", cb, bb, preferred_element_type=jnp.float32)
    weights = (decay * scores[:, None]).astype(jnp.bfloat16)
    parts = jnp.einsum("bhts,bshp->bthp", weights, xb, preferred_element_type=jnp.float32)
    pieces_out = [parts[0]]
    for b in range(1, blocks):
        carried = jnp.einsum(
            "tn,hpn->thp", cb[b].astype(jnp.float32), before[b], precision=lax.Precision.HIGHEST
        )
        pieces_out.append(parts[b] + carried * jnp.exp(cum[b])[:, :, None])
    parts = jnp.concatenate(pieces_out, axis=0)

    correction = jnp.einsum(
        "tn,hpn->thp", c_val.astype(jnp.float32), incoming, precision=lax.Precision.HIGHEST
    )
    parts = (parts + correction * jnp.exp(cum_range)[:, :, None]).reshape(rows, inner)
    y_val = parts / nstate + jnp.repeat(skip_gain, head_dim)[None, :] * x_conv.astype(jnp.float32)
    gated = y_val * jax.nn.silu(z_val.astype(jnp.float32))
    scaled = (gated * norm_gain[None, :]).astype(jnp.bfloat16)
    partial_t = lax.dot_general(
        w_out_cols, scaled, (((1,), (1,)), ((), ())), preferred_element_type=jnp.float32
    )
    result = jnp.transpose(
        lax.psum_scatter(partial_t.astype(jnp.bfloat16), "head", scatter_dimension=0, tiled=True)
    ).astype(jnp.float32)
    total_sq = lax.psum(jnp.sum(gated * gated, axis=1), "head")
    meansq = total_sq / (inner * lax.axis_size("head"))
    return (result * lax.rsqrt(meansq[:, None] + 1e-05)).astype(jnp.bfloat16)


def solution(mesh):
    return jax.shard_map(
        local,
        mesh=mesh,
        in_specs=(
            P("seq", None),
            P("seq", None, "head"),
            P("seq", None),
            P(None, "head"),
            P(),
            P(None, "head"),
            P(),
            P("seq", "head"),
            P("head"),
            P("head", None, None),
            P("head"),
            P("head", "seq"),
        ),
        out_specs=P("seq", "head"),
        check_vma=False,
    )
```

```python
import functools

import jax
import jax.numpy as jnp
from jax import lax
from jax.experimental import pallas as pl
from jax.experimental.pallas import tpu as pltpu
from jax.sharding import PartitionSpec as P

Q = 256


def passed_along(value, axis, by):
    size = lax.axis_size(axis)
    pairs = [(i, i + by) for i in range(size) if 0 <= i + by < size]
    return lax.ppermute(value, axis, pairs)


def depthwise(whole, kernel):
    whole = whole.astype(jnp.float32)
    length = whole.shape[0] - kernel.shape[0] + 1
    total = jnp.zeros((length, whole.shape[1]), jnp.float32)
    for offset in range(kernel.shape[0]):
        total = total + kernel[offset] * whole[offset : offset + length]
    return jax.nn.silu(total).astype(jnp.bfloat16)


def scan_kernel(count, shifts, msg_ref, dec_ref, sin_ref, out_ref, dec_acc, s_send, a_send, s_recv, a_recv, send_sem, recv_sem):
    me = lax.axis_index("seq")
    hd = lax.axis_index("head")
    barrier = pltpu.get_barrier_semaphore()
    distinct = sorted(set(shifts))
    for d in distinct:
        for peer in ((me + d) % count, (me + count - d) % count):
            pl.semaphore_signal(barrier, inc=1, device_id=(peer, hd), device_id_type=pl.DeviceIdType.MESH)
    pl.semaphore_wait(barrier, 2 * len(distinct))
    copies = []
    for k, d in enumerate(shifts):
        if k == 0:
            s_send[k] = msg_ref[...].astype(s_send.dtype)
            a_send[k] = dec_ref[...]
        else:
            s_send[k] = out_ref[...].astype(s_send.dtype)
            a_send[k] = dec_acc[...]
        target = ((me + d) % count, hd)
        sends = 1 - (me + d) // count
        receives = (me - d + count) // count
        pair = []
        for index, (src, dst) in enumerate(((s_send, s_recv), (a_send, a_recv))):
            copy = pltpu.make_async_remote_copy(
                src_ref=src.at[k],
                dst_ref=dst.at[k],
                send_sem=send_sem.at[index, k],
                recv_sem=recv_sem.at[index, k],
                device_id=target,
                device_id_type=pl.DeviceIdType.MESH,
            )
            pl.when(sends == 1)(copy.start)
            pair.append(copy)
        copies.append((sends, pair))
        for copy in pair:
            pl.when(receives == 1)(copy.wait_recv)
        far_s = s_recv[k].astype(jnp.float32)
        far_a = a_recv[k]
        if k == 0:
            out_ref[...] = jnp.where(me == 0, sin_ref[...], far_s)
            dec_acc[...] = jnp.where(me == 0, jnp.zeros_like(far_a), far_a)
        else:
            acc_s = out_ref[...]
            acc_a = dec_acc[...]
            out_ref[...] = jnp.where(me >= d, acc_a[:, None, :] * far_s + acc_s, acc_s)
            dec_acc[...] = jnp.where(me >= d, acc_a * far_a, acc_a)
    for sends, pair in copies:
        for copy in pair:
            pl.when(sends == 1)(copy.wait_send)


def entering_state(decay, end_state, state_in):
    count = lax.axis_size("seq")
    heads, rows, lanes = end_state.shape
    decay_rows = jnp.broadcast_to(decay[:, None], (heads, lanes))
    shifts = [1]
    step = 1
    while step < count:
        shifts.append(step)
        step *= 2
    steps = len(shifts)
    return pl.pallas_call(
        functools.partial(scan_kernel, count, tuple(shifts)),
        out_shape=jax.ShapeDtypeStruct(end_state.shape, jnp.float32),
        in_specs=[pl.BlockSpec(memory_space=pltpu.VMEM)] * 3,
        out_specs=pl.BlockSpec(memory_space=pltpu.VMEM),
        scratch_shapes=[
            pltpu.VMEM(decay_rows.shape, jnp.float32),
            pltpu.VMEM((steps,) + end_state.shape, jnp.bfloat16),
            pltpu.VMEM((steps,) + decay_rows.shape, jnp.float32),
            pltpu.VMEM((steps,) + end_state.shape, jnp.bfloat16),
            pltpu.VMEM((steps,) + decay_rows.shape, jnp.float32),
            pltpu.SemaphoreType.DMA((2, steps)),
            pltpu.SemaphoreType.DMA((2, steps)),
        ],
        compiler_params=pltpu.CompilerParams(collective_id=0, has_side_effects=True),
    )(end_state, decay_rows, state_in)


def local(
    tokens,
    w_xz,
    w_bc,
    conv_x,
    conv_bc,
    tail_x,
    tail_bc,
    decay_code,
    skip_gain,
    state_in,
    norm_gain,
    w_out,
):
    rows = tokens.shape[0]
    heads, head_dim, nstate = state_in.shape
    inner = heads * head_dim
    seq_count = lax.axis_size("seq")
    first = lax.axis_index("seq") == 0
    w_x = w_xz[:, 0, :]
    w_z = w_xz[:, 1, :]
    packed = jnp.concatenate([w_x, w_z, w_bc], axis=1)
    gathered = lax.all_gather(packed, "seq", axis=0, tiled=True)
    w_out_cols = lax.all_gather(jnp.transpose(w_out), "seq", axis=0, tiled=True)
    lag = conv_x.shape[0] - 1
    earlier = passed_along(tokens[rows - lag :], "seq", 1)
    extended = jnp.concatenate([earlier, tokens], axis=0)
    xzbc = jnp.dot(extended, gathered, preferred_element_type=jnp.float32).astype(jnp.bfloat16)
    opening = lax.broadcasted_iota(jnp.int32, (rows + lag, 1), 0) < lag
    whole_x = jnp.where(first & opening, jnp.pad(tail_x, ((0, rows), (0, 0))), xzbc[:, :inner])
    whole_bc = jnp.where(first & opening, jnp.pad(tail_bc, ((0, rows), (0, 0))), xzbc[:, 2 * inner :])
    z_val = xzbc[lag:, inner : 2 * inner]
    x_conv = depthwise(whole_x, conv_x)
    bc_conv = depthwise(whole_bc, conv_bc)
    b_val = bc_conv[:, :nstate]
    c_val = bc_conv[:, nstate:]
    logdec = -decay_code.astype(jnp.float32) / (16.0 * rows * seq_count)
    blocks = rows // Q
    xb = x_conv.reshape(blocks, Q, heads, head_dim)
    bb = b_val.reshape(blocks, Q, nstate)
    cb = c_val.reshape(blocks, Q, nstate)
    cum = jnp.cumsum(logdec.reshape(blocks, Q, heads), axis=1)

    tail_decay = jnp.exp(cum[:, -1:, :] - cum)
    decayed_b = (
        jnp.transpose(tail_decay, (0, 2, 1))[..., None] * bb.astype(jnp.float32)[:, None]
    ).astype(jnp.bfloat16)
    added = jnp.einsum("bhsn,bshp->bhpn", decayed_b, xb, preferred_element_type=jnp.float32)
    block_decay = jnp.exp(cum[:, -1, :])
    before = [None]
    running = added[0]
    for b in range(1, blocks):
        before.append(running)
        running = block_decay[b][:, None, None] * running + added[b]
    cum_range = jnp.cumsum(logdec, axis=0)
    range_decay = jnp.exp(cum_range[-1])
    incoming = entering_state(range_decay, running, state_in)

    places = jnp.arange(Q)
    lower = places[:, None] >= places[None, :]
    cumt = jnp.transpose(cum, (0, 2, 1))
    diff = cumt[:, :, :, None] - cumt[:, :, None, :]
    decay = jnp.where(lower, jnp.exp(jnp.where(lower, diff, 0.0)), 0.0)
    scores = jnp.einsum("btn,bsn->bts", cb, bb, preferred_element_type=jnp.float32)
    weights = (decay * scores[:, None]).astype(jnp.bfloat16)
    parts = jnp.einsum("bhts,bshp->bthp", weights, xb, preferred_element_type=jnp.float32)
    pieces_out = [parts[0]]
    for b in range(1, blocks):
        carried = jnp.einsum(
            "tn,hpn->thp", cb[b].astype(jnp.float32), before[b], precision=lax.Precision.HIGHEST
        )
        pieces_out.append(parts[b] + carried * jnp.exp(cum[b])[:, :, None])
    parts = jnp.concatenate(pieces_out, axis=0)

    correction = jnp.einsum(
        "tn,hpn->thp", c_val.astype(jnp.float32), incoming, precision=lax.Precision.HIGHEST
    )
    parts = (parts + correction * jnp.exp(cum_range)[:, :, None]).reshape(rows, inner)
    y_val = parts / nstate + jnp.repeat(skip_gain, head_dim)[None, :] * x_conv.astype(jnp.float32)
    gated = y_val * jax.nn.silu(z_val.astype(jnp.float32))
    scaled = (gated * norm_gain[None, :]).astype(jnp.bfloat16)
    partial_t = lax.dot_general(
        w_out_cols, scaled, (((1,), (1,)), ((), ())), preferred_element_type=jnp.float32
    )
    result = jnp.transpose(
        lax.psum_scatter(partial_t.astype(jnp.bfloat16), "head", scatter_dimension=0, tiled=True)
    ).astype(jnp.float32)
    total_sq = lax.psum(jnp.sum(gated * gated, axis=1), "head")
    meansq = total_sq / (inner * lax.axis_size("head"))
    return (result * lax.rsqrt(meansq[:, None] + 1e-05)).astype(jnp.bfloat16)


def solution(mesh):
    return jax.shard_map(
        local,
        mesh=mesh,
        in_specs=(
            P("seq", None),
            P("seq", None, "head"),
            P("seq", None),
            P(None, "head"),
            P(),
            P(None, "head"),
            P(),
            P("seq", "head"),
            P("head"),
            P("head", None, None),
            P("head"),
            P("head", "seq"),
        ),
        out_specs=P("seq", "head"),
        check_vma=False,
    )
```

```python
import functools

import jax
import jax.numpy as jnp
from jax import lax
from jax.experimental import pallas as pl
from jax.experimental.pallas import tpu as pltpu
from jax.sharding import PartitionSpec as P

Q = 256


def passed_along(value, axis, by):
    size = lax.axis_size(axis)
    pairs = [(i, i + by) for i in range(size) if 0 <= i + by < size]
    return lax.ppermute(value, axis, pairs)


def depthwise(whole, kernel):
    whole = whole.astype(jnp.float32)
    length = whole.shape[0] - kernel.shape[0] + 1
    total = jnp.zeros((length, whole.shape[1]), jnp.float32)
    for offset in range(kernel.shape[0]):
        total = total + kernel[offset] * whole[offset : offset + length]
    return jax.nn.silu(total).astype(jnp.bfloat16)


def scan_kernel(count, shifts, msg_ref, dec_ref, sin_ref, out_ref, dec_acc, s_send, a_send, s_recv, a_recv, send_sem, recv_sem):
    me = lax.axis_index("seq")
    hd = lax.axis_index("head")
    barrier = pltpu.get_barrier_semaphore()
    distinct = sorted(set(shifts))
    for d in distinct:
        for peer in ((me + d) % count, (me + count - d) % count):
            pl.semaphore_signal(barrier, inc=1, device_id=(peer, hd), device_id_type=pl.DeviceIdType.MESH)
    pl.semaphore_wait(barrier, 2 * len(distinct))
    copies = []
    for k, d in enumerate(shifts):
        if k == 0:
            s_send[k] = msg_ref[...].astype(s_send.dtype)
            a_send[k] = dec_ref[...]
        else:
            s_send[k] = out_ref[...].astype(s_send.dtype)
            a_send[k] = dec_acc[...]
        target = ((me + d) % count, hd)
        sends = 1 - (me + d) // count
        receives = (me - d + count) // count
        pair = []
        for index, (src, dst) in enumerate(((s_send, s_recv), (a_send, a_recv))):
            copy = pltpu.make_async_remote_copy(
                src_ref=src.at[k],
                dst_ref=dst.at[k],
                send_sem=send_sem.at[index, k],
                recv_sem=recv_sem.at[index, k],
                device_id=target,
                device_id_type=pl.DeviceIdType.MESH,
            )
            pl.when(sends == 1)(copy.start)
            pair.append(copy)
        copies.append((sends, pair))
        for copy in pair:
            pl.when(receives == 1)(copy.wait_recv)
        far_s = s_recv[k].astype(jnp.float32)
        far_a = a_recv[k]
        if k == 0:
            out_ref[...] = jnp.where(me == 0, sin_ref[...], far_s)
            dec_acc[...] = jnp.where(me == 0, jnp.zeros_like(far_a), far_a)
        else:
            acc_s = out_ref[...]
            acc_a = dec_acc[...]
            out_ref[...] = jnp.where(me >= d, acc_a[:, None, :] * far_s + acc_s, acc_s)
            dec_acc[...] = jnp.where(me >= d, acc_a * far_a, acc_a)
    for sends, pair in copies:
        for copy in pair:
            pl.when(sends == 1)(copy.wait_send)


def entering_state(decay, end_state, state_in):
    count = lax.axis_size("seq")
    heads, rows, lanes = end_state.shape
    decay_rows = jnp.broadcast_to(decay[:, None], (heads, lanes))
    shifts = [1]
    step = 1
    while step < count:
        shifts.append(step)
        step *= 2
    steps = len(shifts)
    return pl.pallas_call(
        functools.partial(scan_kernel, count, tuple(shifts)),
        out_shape=jax.ShapeDtypeStruct(end_state.shape, jnp.float32),
        in_specs=[pl.BlockSpec(memory_space=pltpu.VMEM)] * 3,
        out_specs=pl.BlockSpec(memory_space=pltpu.VMEM),
        scratch_shapes=[
            pltpu.VMEM(decay_rows.shape, jnp.float32),
            pltpu.VMEM((steps,) + end_state.shape, jnp.bfloat16),
            pltpu.VMEM((steps,) + decay_rows.shape, jnp.float32),
            pltpu.VMEM((steps,) + end_state.shape, jnp.bfloat16),
            pltpu.VMEM((steps,) + decay_rows.shape, jnp.float32),
            pltpu.SemaphoreType.DMA((2, steps)),
            pltpu.SemaphoreType.DMA((2, steps)),
        ],
        compiler_params=pltpu.CompilerParams(collective_id=0, has_side_effects=True),
    )(end_state, decay_rows, state_in)


def local(
    tokens,
    w_xz,
    w_bc,
    conv_x,
    conv_bc,
    tail_x,
    tail_bc,
    decay_code,
    skip_gain,
    state_in,
    norm_gain,
    w_out,
):
    rows = tokens.shape[0]
    heads, head_dim, nstate = state_in.shape
    inner = heads * head_dim
    seq_count = lax.axis_size("seq")
    first = lax.axis_index("seq") == 0
    w_x = w_xz[:, 0, :]
    w_z = w_xz[:, 1, :]
    core = lax.axis_index("head") % 2
    half = w_bc.shape[1] // 2
    w_half = jnp.where(core == 0, w_bc[:, :half], w_bc[:, half:])
    packed = jnp.concatenate([w_x, w_z, w_half], axis=1)
    gathered = lax.all_gather(packed, "seq", axis=0, tiled=True)
    w_out_cols = lax.all_gather(jnp.transpose(w_out), "seq", axis=0, tiled=True)
    lag = conv_x.shape[0] - 1
    earlier = passed_along(tokens[rows - lag :], "seq", 1)
    extended = jnp.concatenate([earlier, tokens], axis=0)
    xzbc = jnp.dot(extended, gathered, preferred_element_type=jnp.float32).astype(jnp.bfloat16)
    own_half = xzbc[:, 2 * inner :]
    heads_count = lax.axis_size("head")
    other_half = lax.ppermute(own_half, "head", [(i, i ^ 1) for i in range(heads_count)])
    bc_all = jnp.where(
        core == 0,
        jnp.concatenate([own_half, other_half], axis=1),
        jnp.concatenate([other_half, own_half], axis=1),
    )
    opening = lax.broadcasted_iota(jnp.int32, (rows + lag, 1), 0) < lag
    whole_x = jnp.where(first & opening, jnp.pad(tail_x, ((0, rows), (0, 0))), xzbc[:, :inner])
    whole_bc = jnp.where(first & opening, jnp.pad(tail_bc, ((0, rows), (0, 0))), bc_all)
    z_val = xzbc[lag:, inner : 2 * inner]
    x_conv = depthwise(whole_x, conv_x)
    bc_conv = depthwise(whole_bc, conv_bc)
    b_val = bc_conv[:, :nstate]
    c_val = bc_conv[:, nstate:]
    logdec = -decay_code.astype(jnp.float32) / (16.0 * rows * seq_count)
    blocks = rows // Q
    xb = x_conv.reshape(blocks, Q, heads, head_dim)
    bb = b_val.reshape(blocks, Q, nstate)
    cb = c_val.reshape(blocks, Q, nstate)
    cum = jnp.cumsum(logdec.reshape(blocks, Q, heads), axis=1)

    tail_decay = jnp.exp(cum[:, -1:, :] - cum)
    decayed_b = (
        jnp.transpose(tail_decay, (0, 2, 1))[..., None] * bb.astype(jnp.float32)[:, None]
    ).astype(jnp.bfloat16)
    added = jnp.einsum("bhsn,bshp->bhpn", decayed_b, xb, preferred_element_type=jnp.float32)
    block_decay = jnp.exp(cum[:, -1, :])
    before = [None]
    running = added[0]
    for b in range(1, blocks):
        before.append(running)
        running = block_decay[b][:, None, None] * running + added[b]
    cum_range = jnp.cumsum(logdec, axis=0)
    range_decay = jnp.exp(cum_range[-1])
    incoming = entering_state(range_decay, running, state_in)

    places = jnp.arange(Q)
    lower = places[:, None] >= places[None, :]
    cumt = jnp.transpose(cum, (0, 2, 1))
    diff = cumt[:, :, :, None] - cumt[:, :, None, :]
    decay = jnp.where(lower, jnp.exp(jnp.where(lower, diff, 0.0)), 0.0)
    scores = jnp.einsum("btn,bsn->bts", cb, bb, preferred_element_type=jnp.float32)
    weights = (decay * scores[:, None]).astype(jnp.bfloat16)
    parts = jnp.einsum("bhts,bshp->bthp", weights, xb, preferred_element_type=jnp.float32)
    pieces_out = [parts[0]]
    for b in range(1, blocks):
        carried = jnp.einsum(
            "tn,hpn->thp", cb[b].astype(jnp.float32), before[b], precision=lax.Precision.HIGHEST
        )
        pieces_out.append(parts[b] + carried * jnp.exp(cum[b])[:, :, None])
    parts = jnp.concatenate(pieces_out, axis=0)

    correction = jnp.einsum(
        "tn,hpn->thp", c_val.astype(jnp.float32), incoming, precision=lax.Precision.HIGHEST
    )
    parts = (parts + correction * jnp.exp(cum_range)[:, :, None]).reshape(rows, inner)
    y_val = parts / nstate + jnp.repeat(skip_gain, head_dim)[None, :] * x_conv.astype(jnp.float32)
    gated = y_val * jax.nn.silu(z_val.astype(jnp.float32))
    scaled = (gated * norm_gain[None, :]).astype(jnp.bfloat16)
    partial_t = lax.dot_general(
        w_out_cols, scaled, (((1,), (1,)), ((), ())), preferred_element_type=jnp.float32
    )
    result = jnp.transpose(
        lax.psum_scatter(partial_t.astype(jnp.bfloat16), "head", scatter_dimension=0, tiled=True)
    ).astype(jnp.float32)
    total_sq = lax.psum(jnp.sum(gated * gated, axis=1), "head")
    meansq = total_sq / (inner * lax.axis_size("head"))
    return (result * lax.rsqrt(meansq[:, None] + 1e-05)).astype(jnp.bfloat16)


def solution(mesh):
    return jax.shard_map(
        local,
        mesh=mesh,
        in_specs=(
            P("seq", None),
            P("seq", None, "head"),
            P("seq", None),
            P(None, "head"),
            P(),
            P(None, "head"),
            P(),
            P("seq", "head"),
            P("head"),
            P("head", None, None),
            P("head"),
            P("head", "seq"),
        ),
        out_specs=P("seq", "head"),
        check_vma=False,
    )
```

```python
import functools

import jax
import jax.numpy as jnp
from jax import lax
from jax.experimental import pallas as pl
from jax.experimental.pallas import tpu as pltpu
from jax.sharding import PartitionSpec as P

Q = 256


def passed_along(value, axis, by):
    size = lax.axis_size(axis)
    pairs = [(i, i + by) for i in range(size) if 0 <= i + by < size]
    return lax.ppermute(value, axis, pairs)


def depthwise(whole, kernel):
    whole = whole.astype(jnp.float32)
    length = whole.shape[0] - kernel.shape[0] + 1
    total = jnp.zeros((length, whole.shape[1]), jnp.float32)
    for offset in range(kernel.shape[0]):
        total = total + kernel[offset] * whole[offset : offset + length]
    return jax.nn.silu(total).astype(jnp.bfloat16)


def scan_kernel(count, shifts, msg_ref, dec_ref, sin_ref, out_ref, dec_acc, s_send, a_send, s_recv, a_recv, send_sem, recv_sem):
    me = lax.axis_index("seq")
    hd = lax.axis_index("head")
    barrier = pltpu.get_barrier_semaphore()
    distinct = sorted(set(shifts))
    for d in distinct:
        for peer in ((me + d) % count, (me + count - d) % count):
            pl.semaphore_signal(barrier, inc=1, device_id=(peer, hd), device_id_type=pl.DeviceIdType.MESH)
    pl.semaphore_wait(barrier, 2 * len(distinct))
    copies = []
    for k, d in enumerate(shifts):
        if k == 0:
            s_send[k] = msg_ref[...].astype(s_send.dtype)
            a_send[k] = dec_ref[...]
        else:
            s_send[k] = out_ref[...].astype(s_send.dtype)
            a_send[k] = dec_acc[...]
        target = ((me + d) % count, hd)
        sends = 1 - (me + d) // count
        receives = (me - d + count) // count
        pair = []
        for index, (src, dst) in enumerate(((s_send, s_recv), (a_send, a_recv))):
            copy = pltpu.make_async_remote_copy(
                src_ref=src.at[k],
                dst_ref=dst.at[k],
                send_sem=send_sem.at[index, k],
                recv_sem=recv_sem.at[index, k],
                device_id=target,
                device_id_type=pl.DeviceIdType.MESH,
            )
            pl.when(sends == 1)(copy.start)
            pair.append(copy)
        copies.append((sends, pair))
        for copy in pair:
            pl.when(receives == 1)(copy.wait_recv)
        far_s = s_recv[k].astype(jnp.float32)
        far_a = a_recv[k]
        if k == 0:
            out_ref[...] = jnp.where(me == 0, sin_ref[...], far_s)
            dec_acc[...] = jnp.where(me == 0, jnp.zeros_like(far_a), far_a)
        else:
            acc_s = out_ref[...]
            acc_a = dec_acc[...]
            out_ref[...] = jnp.where(me >= d, acc_a[:, None, :] * far_s + acc_s, acc_s)
            dec_acc[...] = jnp.where(me >= d, acc_a * far_a, acc_a)
    for sends, pair in copies:
        for copy in pair:
            pl.when(sends == 1)(copy.wait_send)


def entering_state(decay, end_state, state_in):
    count = lax.axis_size("seq")
    heads, rows, lanes = end_state.shape
    decay_rows = jnp.broadcast_to(decay[:, None], (heads, lanes))
    shifts = [1]
    step = 1
    while step < count:
        shifts.append(step)
        step *= 2
    steps = len(shifts)
    return pl.pallas_call(
        functools.partial(scan_kernel, count, tuple(shifts)),
        out_shape=jax.ShapeDtypeStruct(end_state.shape, jnp.float32),
        in_specs=[pl.BlockSpec(memory_space=pltpu.VMEM)] * 3,
        out_specs=pl.BlockSpec(memory_space=pltpu.VMEM),
        scratch_shapes=[
            pltpu.VMEM(decay_rows.shape, jnp.float32),
            pltpu.VMEM((steps,) + end_state.shape, jnp.bfloat16),
            pltpu.VMEM((steps,) + decay_rows.shape, jnp.float32),
            pltpu.VMEM((steps,) + end_state.shape, jnp.bfloat16),
            pltpu.VMEM((steps,) + decay_rows.shape, jnp.float32),
            pltpu.SemaphoreType.DMA((2, steps)),
            pltpu.SemaphoreType.DMA((2, steps)),
        ],
        compiler_params=pltpu.CompilerParams(collective_id=0, has_side_effects=True),
    )(end_state, decay_rows, state_in)


def local(
    tokens,
    w_xz,
    w_bc,
    conv_x,
    conv_bc,
    tail_x,
    tail_bc,
    decay_code,
    skip_gain,
    state_in,
    norm_gain,
    w_out,
):
    rows = tokens.shape[0]
    heads, head_dim, nstate = state_in.shape
    inner = heads * head_dim
    seq_count = lax.axis_size("seq")
    first = lax.axis_index("seq") == 0
    w_x = w_xz[:, 0, :]
    w_z = w_xz[:, 1, :]
    heads_count = lax.axis_size("head")
    hindex = lax.axis_index("head")
    core = hindex % 2
    chip = hindex // 2
    chips = heads_count // 2
    width = w_bc.shape[1] // heads_count
    w_half = lax.dynamic_slice_in_dim(w_bc, hindex * width, width, axis=1)
    packed = jnp.concatenate([w_x, w_z, w_half], axis=1)
    gathered = lax.all_gather(packed, "seq", axis=0, tiled=True)
    w_out_cols = lax.all_gather(jnp.transpose(w_out), "seq", axis=0, tiled=True)
    lag = conv_x.shape[0] - 1
    earlier = passed_along(tokens[rows - lag :], "seq", 1)
    extended = jnp.concatenate([earlier, tokens], axis=0)
    xzbc = jnp.dot(extended, gathered, preferred_element_type=jnp.float32).astype(jnp.bfloat16)
    own_part = xzbc[:, 2 * inner :]
    other_part = lax.ppermute(own_part, "head", [(i, i ^ 1) for i in range(heads_count)])
    chip_piece = jnp.where(
        core == 0,
        jnp.concatenate([own_part, other_part], axis=1),
        jnp.concatenate([other_part, own_part], axis=1),
    )
    received = [chip_piece] + [
        lax.ppermute(chip_piece, "head", [(i, (i + 2 * k) % heads_count) for i in range(heads_count)])
        for k in range(1, chips)
    ]
    stacked = jnp.stack(received)
    bc_all = jnp.concatenate(
        [lax.dynamic_index_in_dim(stacked, (chip - j + chips) % chips, keepdims=False) for j in range(chips)],
        axis=1,
    )
    opening = lax.broadcasted_iota(jnp.int32, (rows + lag, 1), 0) < lag
    whole_x = jnp.where(first & opening, jnp.pad(tail_x, ((0, rows), (0, 0))), xzbc[:, :inner])
    whole_bc = jnp.where(first & opening, jnp.pad(tail_bc, ((0, rows), (0, 0))), bc_all)
    z_val = xzbc[lag:, inner : 2 * inner]
    x_conv = depthwise(whole_x, conv_x)
    bc_conv = depthwise(whole_bc, conv_bc)
    b_val = bc_conv[:, :nstate]
    c_val = bc_conv[:, nstate:]
    logdec = -decay_code.astype(jnp.float32) / (16.0 * rows * seq_count)
    blocks = rows // Q
    xb = x_conv.reshape(blocks, Q, heads, head_dim)
    bb = b_val.reshape(blocks, Q, nstate)
    cb = c_val.reshape(blocks, Q, nstate)
    cum = jnp.cumsum(logdec.reshape(blocks, Q, heads), axis=1)

    tail_decay = jnp.exp(cum[:, -1:, :] - cum)
    decayed_b = (
        jnp.transpose(tail_decay, (0, 2, 1))[..., None] * bb.astype(jnp.float32)[:, None]
    ).astype(jnp.bfloat16)
    added = jnp.einsum("bhsn,bshp->bhpn", decayed_b, xb, preferred_element_type=jnp.float32)
    block_decay = jnp.exp(cum[:, -1, :])
    before = [None]
    running = added[0]
    for b in range(1, blocks):
        before.append(running)
        running = block_decay[b][:, None, None] * running + added[b]
    cum_range = jnp.cumsum(logdec, axis=0)
    range_decay = jnp.exp(cum_range[-1])
    incoming = entering_state(range_decay, running, state_in)

    places = jnp.arange(Q)
    lower = places[:, None] >= places[None, :]
    cumt = jnp.transpose(cum, (0, 2, 1))
    diff = cumt[:, :, :, None] - cumt[:, :, None, :]
    decay = jnp.where(lower, jnp.exp(jnp.where(lower, diff, 0.0)), 0.0)
    scores = jnp.einsum("btn,bsn->bts", cb, bb, preferred_element_type=jnp.float32)
    weights = (decay * scores[:, None]).astype(jnp.bfloat16)
    parts = jnp.einsum("bhts,bshp->bthp", weights, xb, preferred_element_type=jnp.float32)
    pieces_out = [parts[0]]
    for b in range(1, blocks):
        carried = jnp.einsum(
            "tn,hpn->thp", cb[b].astype(jnp.float32), before[b], precision=lax.Precision.HIGHEST
        )
        pieces_out.append(parts[b] + carried * jnp.exp(cum[b])[:, :, None])
    parts = jnp.concatenate(pieces_out, axis=0)

    correction = jnp.einsum(
        "tn,hpn->thp", c_val.astype(jnp.float32), incoming, precision=lax.Precision.HIGHEST
    )
    parts = (parts + correction * jnp.exp(cum_range)[:, :, None]).reshape(rows, inner)
    y_val = parts / nstate + jnp.repeat(skip_gain, head_dim)[None, :] * x_conv.astype(jnp.float32)
    gated = y_val * jax.nn.silu(z_val.astype(jnp.float32))
    scaled = (gated * norm_gain[None, :]).astype(jnp.bfloat16)
    partial_t = lax.dot_general(
        w_out_cols, scaled, (((1,), (1,)), ((), ())), preferred_element_type=jnp.float32
    )
    result = jnp.transpose(
        lax.psum_scatter(partial_t.astype(jnp.bfloat16), "head", scatter_dimension=0, tiled=True)
    ).astype(jnp.float32)
    total_sq = lax.psum(jnp.sum(gated * gated, axis=1), "head")
    meansq = total_sq / (inner * lax.axis_size("head"))
    return (result * lax.rsqrt(meansq[:, None] + 1e-05)).astype(jnp.bfloat16)


def solution(mesh):
    return jax.shard_map(
        local,
        mesh=mesh,
        in_specs=(
            P("seq", None),
            P("seq", None, "head"),
            P("seq", None),
            P(None, "head"),
            P(),
            P(None, "head"),
            P(),
            P("seq", "head"),
            P("head"),
            P("head", None, None),
            P("head"),
            P("head", "seq"),
        ),
        out_specs=P("seq", "head"),
        check_vma=False,
    )
```

```python
import functools

import jax
import jax.numpy as jnp
from jax import lax
from jax.experimental import pallas as pl
from jax.experimental.pallas import tpu as pltpu
from jax.sharding import Mesh, PartitionSpec as P

Q = 256


HEAD = ("hy", "hc")


def head_size():
    return lax.axis_size("hy") * lax.axis_size("hc")


def passed_along(value, axis, by):
    size = lax.axis_size(axis)
    pairs = [(i, i + by) for i in range(size) if 0 <= i + by < size]
    return lax.ppermute(value, axis, pairs)


def depthwise(whole, kernel):
    whole = whole.astype(jnp.float32)
    length = whole.shape[0] - kernel.shape[0] + 1
    total = jnp.zeros((length, whole.shape[1]), jnp.float32)
    for offset in range(kernel.shape[0]):
        total = total + kernel[offset] * whole[offset : offset + length]
    return jax.nn.silu(total).astype(jnp.bfloat16)


def scan_kernel(count, shifts, msg_ref, dec_ref, sin_ref, out_ref, dec_acc, s_send, a_send, s_recv, a_recv, send_sem, recv_sem):
    me = lax.axis_index("seq")
    hy = lax.axis_index("hy")
    hc = lax.axis_index("hc")
    barrier = pltpu.get_barrier_semaphore()
    distinct = sorted(set(shifts))
    for d in distinct:
        for peer in ((me + d) % count, (me + count - d) % count):
            pl.semaphore_signal(barrier, inc=1, device_id=(peer, hy, hc), device_id_type=pl.DeviceIdType.MESH)
    pl.semaphore_wait(barrier, 2 * len(distinct))
    copies = []
    for k, d in enumerate(shifts):
        if k == 0:
            s_send[k] = msg_ref[...].astype(s_send.dtype)
            a_send[k] = dec_ref[...]
        else:
            s_send[k] = out_ref[...].astype(s_send.dtype)
            a_send[k] = dec_acc[...]
        target = ((me + d) % count, hy, hc)
        sends = 1 - (me + d) // count
        receives = (me - d + count) // count
        pair = []
        for index, (src, dst) in enumerate(((s_send, s_recv), (a_send, a_recv))):
            copy = pltpu.make_async_remote_copy(
                src_ref=src.at[k],
                dst_ref=dst.at[k],
                send_sem=send_sem.at[index, k],
                recv_sem=recv_sem.at[index, k],
                device_id=target,
                device_id_type=pl.DeviceIdType.MESH,
            )
            pl.when(sends == 1)(copy.start)
            pair.append(copy)
        copies.append((sends, pair))
        for copy in pair:
            pl.when(receives == 1)(copy.wait_recv)
        far_s = s_recv[k].astype(jnp.float32)
        far_a = a_recv[k]
        if k == 0:
            out_ref[...] = jnp.where(me == 0, sin_ref[...], far_s)
            dec_acc[...] = jnp.where(me == 0, jnp.zeros_like(far_a), far_a)
        else:
            acc_s = out_ref[...]
            acc_a = dec_acc[...]
            out_ref[...] = jnp.where(me >= d, acc_a[:, None, :] * far_s + acc_s, acc_s)
            dec_acc[...] = jnp.where(me >= d, acc_a * far_a, acc_a)
    for sends, pair in copies:
        for copy in pair:
            pl.when(sends == 1)(copy.wait_send)


def entering_state(decay, end_state, state_in):
    count = lax.axis_size("seq")
    heads, rows, lanes = end_state.shape
    decay_rows = jnp.broadcast_to(decay[:, None], (heads, lanes))
    shifts = [1]
    step = 1
    while step < count:
        shifts.append(step)
        step *= 2
    steps = len(shifts)
    return pl.pallas_call(
        functools.partial(scan_kernel, count, tuple(shifts)),
        out_shape=jax.ShapeDtypeStruct(end_state.shape, jnp.float32),
        in_specs=[pl.BlockSpec(memory_space=pltpu.VMEM)] * 3,
        out_specs=pl.BlockSpec(memory_space=pltpu.VMEM),
        scratch_shapes=[
            pltpu.VMEM(decay_rows.shape, jnp.float32),
            pltpu.VMEM((steps,) + end_state.shape, jnp.bfloat16),
            pltpu.VMEM((steps,) + decay_rows.shape, jnp.float32),
            pltpu.VMEM((steps,) + end_state.shape, jnp.bfloat16),
            pltpu.VMEM((steps,) + decay_rows.shape, jnp.float32),
            pltpu.SemaphoreType.DMA((2, steps)),
            pltpu.SemaphoreType.DMA((2, steps)),
        ],
        compiler_params=pltpu.CompilerParams(collective_id=0, has_side_effects=True),
    )(end_state, decay_rows, state_in)


def local(
    tokens,
    w_xz,
    w_bc,
    conv_x,
    conv_bc,
    tail_x,
    tail_bc,
    decay_code,
    skip_gain,
    state_in,
    norm_gain,
    w_out,
):
    rows = tokens.shape[0]
    heads, head_dim, nstate = state_in.shape
    inner = heads * head_dim
    seq_count = lax.axis_size("seq")
    first = lax.axis_index("seq") == 0
    w_x = w_xz[:, 0, :]
    w_z = w_xz[:, 1, :]
    heads_count = head_size()
    hindex = lax.axis_index(HEAD)
    core = hindex % 2
    chip = hindex // 2
    chips = heads_count // 2
    width = w_bc.shape[1] // heads_count
    w_half = lax.dynamic_slice_in_dim(w_bc, hindex * width, width, axis=1)
    packed = jnp.concatenate([w_x, w_z, w_half], axis=1)
    gathered = lax.all_gather(packed, "seq", axis=0, tiled=True)
    w_out_cols = lax.all_gather(jnp.transpose(w_out), "seq", axis=0, tiled=True)
    lag = conv_x.shape[0] - 1
    earlier = passed_along(tokens[rows - lag :], "seq", 1)
    extended = jnp.concatenate([earlier, tokens], axis=0)
    xzbc = jnp.dot(extended, gathered, preferred_element_type=jnp.float32).astype(jnp.bfloat16)
    own_part = xzbc[:, 2 * inner :]
    other_part = lax.ppermute(own_part, HEAD, [(i, i ^ 1) for i in range(heads_count)])
    chip_piece = jnp.where(
        core == 0,
        jnp.concatenate([own_part, other_part], axis=1),
        jnp.concatenate([other_part, own_part], axis=1),
    )
    received = [chip_piece] + [
        lax.ppermute(chip_piece, HEAD, [(i, (i + 2 * k) % heads_count) for i in range(heads_count)])
        for k in range(1, chips)
    ]
    stacked = jnp.stack(received)
    bc_all = jnp.concatenate(
        [lax.dynamic_index_in_dim(stacked, (chip - j + chips) % chips, keepdims=False) for j in range(chips)],
        axis=1,
    )
    opening = lax.broadcasted_iota(jnp.int32, (rows + lag, 1), 0) < lag
    whole_x = jnp.where(first & opening, jnp.pad(tail_x, ((0, rows), (0, 0))), xzbc[:, :inner])
    whole_bc = jnp.where(first & opening, jnp.pad(tail_bc, ((0, rows), (0, 0))), bc_all)
    z_val = xzbc[lag:, inner : 2 * inner]
    x_conv = depthwise(whole_x, conv_x)
    bc_conv = depthwise(whole_bc, conv_bc)
    b_val = bc_conv[:, :nstate]
    c_val = bc_conv[:, nstate:]
    logdec = -decay_code.astype(jnp.float32) / (16.0 * rows * seq_count)
    blocks = rows // Q
    xb = x_conv.reshape(blocks, Q, heads, head_dim)
    bb = b_val.reshape(blocks, Q, nstate)
    cb = c_val.reshape(blocks, Q, nstate)
    cum = jnp.cumsum(logdec.reshape(blocks, Q, heads), axis=1)

    tail_decay = jnp.exp(cum[:, -1:, :] - cum)
    decayed_b = (
        jnp.transpose(tail_decay, (0, 2, 1))[..., None] * bb.astype(jnp.float32)[:, None]
    ).astype(jnp.bfloat16)
    added = jnp.einsum("bhsn,bshp->bhpn", decayed_b, xb, preferred_element_type=jnp.float32)
    block_decay = jnp.exp(cum[:, -1, :])
    before = [None]
    running = added[0]
    for b in range(1, blocks):
        before.append(running)
        running = block_decay[b][:, None, None] * running + added[b]
    cum_range = jnp.cumsum(logdec, axis=0)
    range_decay = jnp.exp(cum_range[-1])
    incoming = entering_state(range_decay, running, state_in)

    places = jnp.arange(Q)
    lower = places[:, None] >= places[None, :]
    cumt = jnp.transpose(cum, (0, 2, 1))
    diff = cumt[:, :, :, None] - cumt[:, :, None, :]
    decay = jnp.where(lower, jnp.exp(jnp.where(lower, diff, 0.0)), 0.0)
    scores = jnp.einsum("btn,bsn->bts", cb, bb, preferred_element_type=jnp.float32)
    weights = (decay * scores[:, None]).astype(jnp.bfloat16)
    parts = jnp.einsum("bhts,bshp->bthp", weights, xb, preferred_element_type=jnp.float32)
    pieces_out = [parts[0]]
    for b in range(1, blocks):
        carried = jnp.einsum(
            "tn,hpn->thp", cb[b].astype(jnp.float32), before[b], precision=lax.Precision.HIGHEST
        )
        pieces_out.append(parts[b] + carried * jnp.exp(cum[b])[:, :, None])
    parts = jnp.concatenate(pieces_out, axis=0)

    correction = jnp.einsum(
        "tn,hpn->thp", c_val.astype(jnp.float32), incoming, precision=lax.Precision.HIGHEST
    )
    parts = (parts + correction * jnp.exp(cum_range)[:, :, None]).reshape(rows, inner)
    y_val = parts / nstate + jnp.repeat(skip_gain, head_dim)[None, :] * x_conv.astype(jnp.float32)
    gated = y_val * jax.nn.silu(z_val.astype(jnp.float32))
    scaled = (gated * norm_gain[None, :]).astype(jnp.bfloat16)
    cores = lax.axis_size("hc")
    mine = lax.axis_index("hc")
    blocks = w_out_cols.reshape(lax.axis_size("hy"), cores, -1, w_out_cols.shape[1])
    w_mine = lax.dynamic_index_in_dim(blocks, mine, axis=1, keepdims=False)
    w_other = lax.dynamic_index_in_dim(blocks, 1 - mine, axis=1, keepdims=False)
    numbers = (((2,), (1,)), ((), ()))
    kept = lax.dot_general(w_mine, scaled, numbers, preferred_element_type=jnp.float32)
    sent = lax.dot_general(w_other, scaled, numbers, preferred_element_type=jnp.float32).astype(jnp.bfloat16)
    got = lax.ppermute(sent, "hc", [(i, (i + 1) % cores) for i in range(cores)])
    chip_sum = (kept + got.astype(jnp.float32)).astype(jnp.bfloat16)
    result = jnp.transpose(
        lax.psum_scatter(chip_sum, "hy", scatter_dimension=0, tiled=False)
    ).astype(jnp.float32)
    total_sq = lax.psum(jnp.sum(gated * gated, axis=1), HEAD)
    meansq = total_sq / (inner * head_size())
    return (result * lax.rsqrt(meansq[:, None] + 1e-05)).astype(jnp.bfloat16)


def solution(mesh):
    devices = mesh.devices
    cores = 2 if devices.shape[1] % 2 == 0 else 1
    split = Mesh(devices.reshape(devices.shape[0], devices.shape[1] // cores, cores), ("seq", "hy", "hc"))
    return jax.shard_map(
        local,
        mesh=split,
        in_specs=(
            P("seq", None),
            P("seq", None, HEAD),
            P("seq", None),
            P(None, HEAD),
            P(),
            P(None, HEAD),
            P(),
            P("seq", HEAD),
            P(HEAD),
            P(HEAD, None, None),
            P(HEAD),
            P(HEAD, "seq"),
        ),
        out_specs=P("seq", HEAD),
        check_vma=False,
    )
```

```python
import functools

import jax
import jax.numpy as jnp
from jax import lax
from jax.experimental import pallas as pl
from jax.experimental.pallas import tpu as pltpu
from jax.sharding import PartitionSpec as P

Q = 256


def passed_along(value, axis, by):
    size = lax.axis_size(axis)
    pairs = [(i, i + by) for i in range(size) if 0 <= i + by < size]
    return lax.ppermute(value, axis, pairs)


def depthwise(whole, kernel):
    whole = whole.astype(jnp.float32)
    length = whole.shape[0] - kernel.shape[0] + 1
    total = jnp.zeros((length, whole.shape[1]), jnp.float32)
    for offset in range(kernel.shape[0]):
        total = total + kernel[offset] * whole[offset : offset + length]
    return jax.nn.silu(total).astype(jnp.bfloat16)


def scan_kernel(count, shifts, msg_ref, dec_ref, sin_ref, out_ref, dec_acc, s_send, a_send, s_recv, a_recv, send_sem, recv_sem):
    me = lax.axis_index("seq")
    hd = lax.axis_index("head")
    barrier = pltpu.get_barrier_semaphore()
    distinct = sorted(set(shifts))
    for d in distinct:
        for peer in ((me + d) % count, (me + count - d) % count):
            pl.semaphore_signal(barrier, inc=1, device_id=(peer, hd), device_id_type=pl.DeviceIdType.MESH)
    pl.semaphore_wait(barrier, 2 * len(distinct))
    copies = []
    for k, d in enumerate(shifts):
        if k == 0:
            s_send[k] = msg_ref[...].astype(s_send.dtype)
            a_send[k] = dec_ref[...]
        else:
            s_send[k] = out_ref[...].astype(s_send.dtype)
            a_send[k] = dec_acc[...]
        target = ((me + d) % count, hd)
        sends = 1 - (me + d) // count
        receives = (me - d + count) // count
        pair = []
        for index, (src, dst) in enumerate(((s_send, s_recv), (a_send, a_recv))):
            copy = pltpu.make_async_remote_copy(
                src_ref=src.at[k],
                dst_ref=dst.at[k],
                send_sem=send_sem.at[index, k],
                recv_sem=recv_sem.at[index, k],
                device_id=target,
                device_id_type=pl.DeviceIdType.MESH,
            )
            pl.when(sends == 1)(copy.start)
            pair.append(copy)
        copies.append((sends, pair))
        for copy in pair:
            pl.when(receives == 1)(copy.wait_recv)
        far_s = s_recv[k].astype(jnp.float32)
        far_a = a_recv[k]
        if k == 0:
            out_ref[...] = jnp.where(me == 0, sin_ref[...], far_s)
            dec_acc[...] = jnp.where(me == 0, jnp.zeros_like(far_a), far_a)
        else:
            acc_s = out_ref[...]
            acc_a = dec_acc[...]
            out_ref[...] = jnp.where(me >= d, acc_a[:, None, :] * far_s + acc_s, acc_s)
            dec_acc[...] = jnp.where(me >= d, acc_a * far_a, acc_a)
    for sends, pair in copies:
        for copy in pair:
            pl.when(sends == 1)(copy.wait_send)


def entering_state(decay, end_state, state_in):
    count = lax.axis_size("seq")
    heads, rows, lanes = end_state.shape
    decay_rows = jnp.broadcast_to(decay[:, None], (heads, lanes))
    shifts = [1]
    step = 1
    while step < count:
        shifts.append(step)
        step *= 2
    steps = len(shifts)
    return pl.pallas_call(
        functools.partial(scan_kernel, count, tuple(shifts)),
        out_shape=jax.ShapeDtypeStruct(end_state.shape, jnp.float32),
        in_specs=[pl.BlockSpec(memory_space=pltpu.VMEM)] * 3,
        out_specs=pl.BlockSpec(memory_space=pltpu.VMEM),
        scratch_shapes=[
            pltpu.VMEM(decay_rows.shape, jnp.float32),
            pltpu.VMEM((steps,) + end_state.shape, jnp.bfloat16),
            pltpu.VMEM((steps,) + decay_rows.shape, jnp.float32),
            pltpu.VMEM((steps,) + end_state.shape, jnp.bfloat16),
            pltpu.VMEM((steps,) + decay_rows.shape, jnp.float32),
            pltpu.SemaphoreType.DMA((2, steps)),
            pltpu.SemaphoreType.DMA((2, steps)),
        ],
        compiler_params=pltpu.CompilerParams(collective_id=0, has_side_effects=True),
    )(end_state, decay_rows, state_in)


def local(
    tokens,
    w_xz,
    w_bc,
    conv_x,
    conv_bc,
    tail_x,
    tail_bc,
    decay_code,
    skip_gain,
    state_in,
    norm_gain,
    w_out,
):
    rows = tokens.shape[0]
    heads, head_dim, nstate = state_in.shape
    inner = heads * head_dim
    seq_count = lax.axis_size("seq")
    first = lax.axis_index("seq") == 0
    w_x = w_xz[:, 0, :]
    w_z = w_xz[:, 1, :]
    heads_count = lax.axis_size("head")
    hindex = lax.axis_index("head")
    core = hindex % 2
    chip = hindex // 2
    chips = heads_count // 2
    width = w_bc.shape[1] // heads_count
    w_half = lax.dynamic_slice_in_dim(w_bc, hindex * width, width, axis=1)
    packed = jnp.concatenate([w_x, w_z, w_half, jnp.transpose(w_out)], axis=1)
    gathered_all = lax.all_gather(packed, "seq", axis=0, tiled=True)
    proj = w_x.shape[1] + w_z.shape[1] + w_half.shape[1]
    gathered = gathered_all[:, :proj]
    w_out_cols = gathered_all[:, proj:]
    lag = conv_x.shape[0] - 1
    earlier = passed_along(tokens[rows - lag :], "seq", 1)
    extended = jnp.concatenate([earlier, tokens], axis=0)
    xzbc = jnp.dot(extended, gathered, preferred_element_type=jnp.float32).astype(jnp.bfloat16)
    own_part = xzbc[:, 2 * inner :]
    other_part = lax.ppermute(own_part, "head", [(i, i ^ 1) for i in range(heads_count)])
    chip_piece = jnp.where(
        core == 0,
        jnp.concatenate([own_part, other_part], axis=1),
        jnp.concatenate([other_part, own_part], axis=1),
    )
    received = [chip_piece] + [
        lax.ppermute(chip_piece, "head", [(i, (i + 2 * k) % heads_count) for i in range(heads_count)])
        for k in range(1, chips)
    ]
    stacked = jnp.stack(received)
    bc_all = jnp.concatenate(
        [lax.dynamic_index_in_dim(stacked, (chip - j + chips) % chips, keepdims=False) for j in range(chips)],
        axis=1,
    )
    opening = lax.broadcasted_iota(jnp.int32, (rows + lag, 1), 0) < lag
    whole_x = jnp.where(first & opening, jnp.pad(tail_x, ((0, rows), (0, 0))), xzbc[:, :inner])
    whole_bc = jnp.where(first & opening, jnp.pad(tail_bc, ((0, rows), (0, 0))), bc_all)
    z_val = xzbc[lag:, inner : 2 * inner]
    x_conv = depthwise(whole_x, conv_x)
    bc_conv = depthwise(whole_bc, conv_bc)
    b_val = bc_conv[:, :nstate]
    c_val = bc_conv[:, nstate:]
    logdec = -decay_code.astype(jnp.float32) / (16.0 * rows * seq_count)
    blocks = rows // Q
    xb = x_conv.reshape(blocks, Q, heads, head_dim)
    bb = b_val.reshape(blocks, Q, nstate)
    cb = c_val.reshape(blocks, Q, nstate)
    cum = jnp.cumsum(logdec.reshape(blocks, Q, heads), axis=1)

    tail_decay = jnp.exp(cum[:, -1:, :] - cum)
    decayed_b = (
        jnp.transpose(tail_decay, (0, 2, 1))[..., None] * bb.astype(jnp.float32)[:, None]
    ).astype(jnp.bfloat16)
    added = jnp.einsum("bhsn,bshp->bhpn", decayed_b, xb, preferred_element_type=jnp.float32)
    block_decay = jnp.exp(cum[:, -1, :])
    before = [None]
    running = added[0]
    for b in range(1, blocks):
        before.append(running)
        running = block_decay[b][:, None, None] * running + added[b]
    cum_range = jnp.cumsum(logdec, axis=0)
    range_decay = jnp.exp(cum_range[-1])
    incoming = entering_state(range_decay, running, state_in)

    places = jnp.arange(Q)
    lower = places[:, None] >= places[None, :]
    cumt = jnp.transpose(cum, (0, 2, 1))
    diff = cumt[:, :, :, None] - cumt[:, :, None, :]
    decay = jnp.where(lower, jnp.exp(jnp.where(lower, diff, 0.0)), 0.0)
    scores = jnp.einsum("btn,bsn->bts", cb, bb, preferred_element_type=jnp.float32)
    weights = (decay * scores[:, None]).astype(jnp.bfloat16)
    parts = jnp.einsum("bhts,bshp->bthp", weights, xb, preferred_element_type=jnp.float32)
    pieces_out = [parts[0]]
    for b in range(1, blocks):
        carried = jnp.einsum(
            "tn,hpn->thp", cb[b].astype(jnp.float32), before[b], precision=lax.Precision.HIGHEST
        )
        pieces_out.append(parts[b] + carried * jnp.exp(cum[b])[:, :, None])
    parts = jnp.concatenate(pieces_out, axis=0)

    correction = jnp.einsum(
        "tn,hpn->thp", c_val.astype(jnp.float32), incoming, precision=lax.Precision.HIGHEST
    )
    parts = (parts + correction * jnp.exp(cum_range)[:, :, None]).reshape(rows, inner)
    y_val = parts / nstate + jnp.repeat(skip_gain, head_dim)[None, :] * x_conv.astype(jnp.float32)
    gated = y_val * jax.nn.silu(z_val.astype(jnp.float32))
    scaled = (gated * norm_gain[None, :]).astype(jnp.bfloat16)
    partial_t = lax.dot_general(
        w_out_cols, scaled, (((1,), (1,)), ((), ())), preferred_element_type=jnp.float32
    )
    result = jnp.transpose(
        lax.psum_scatter(partial_t.astype(jnp.bfloat16), "head", scatter_dimension=0, tiled=True)
    ).astype(jnp.float32)
    total_sq = lax.psum(jnp.sum(gated * gated, axis=1), "head")
    meansq = total_sq / (inner * lax.axis_size("head"))
    return (result * lax.rsqrt(meansq[:, None] + 1e-05)).astype(jnp.bfloat16)


def solution(mesh):
    return jax.shard_map(
        local,
        mesh=mesh,
        in_specs=(
            P("seq", None),
            P("seq", None, "head"),
            P("seq", None),
            P(None, "head"),
            P(),
            P(None, "head"),
            P(),
            P("seq", "head"),
            P("head"),
            P("head", None, None),
            P("head"),
            P("head", "seq"),
        ),
        out_specs=P("seq", "head"),
        check_vma=False,
    )
```

```python
import functools

import jax
import jax.numpy as jnp
from jax import lax
from jax.experimental import pallas as pl
from jax.experimental.pallas import tpu as pltpu
from jax.sharding import PartitionSpec as P

Q = 256


def passed_along(value, axis, by):
    size = lax.axis_size(axis)
    pairs = [(i, i + by) for i in range(size) if 0 <= i + by < size]
    return lax.ppermute(value, axis, pairs)


def depthwise(whole, kernel):
    whole = whole.astype(jnp.float32)
    length = whole.shape[0] - kernel.shape[0] + 1
    total = jnp.zeros((length, whole.shape[1]), jnp.float32)
    for offset in range(kernel.shape[0]):
        total = total + kernel[offset] * whole[offset : offset + length]
    return jax.nn.silu(total).astype(jnp.bfloat16)


def scan_kernel(count, shifts, msg_ref, dec_ref, sin_ref, out_ref, dec_acc, s_send, a_send, s_recv, a_recv, send_sem, recv_sem):
    me = lax.axis_index("seq")
    hd = lax.axis_index("head")
    barrier = pltpu.get_barrier_semaphore()
    distinct = sorted(set(shifts))
    for d in distinct:
        for peer in ((me + d) % count, (me + count - d) % count):
            pl.semaphore_signal(barrier, inc=1, device_id=(peer, hd), device_id_type=pl.DeviceIdType.MESH)
    pl.semaphore_wait(barrier, 2 * len(distinct))
    copies = []
    for k, d in enumerate(shifts):
        if k == 0:
            s_send[k] = msg_ref[...].astype(s_send.dtype)
            a_send[k] = dec_ref[...]
        else:
            s_send[k] = out_ref[...].astype(s_send.dtype)
            a_send[k] = dec_acc[...]
        target = ((me + d) % count, hd)
        sends = 1 - (me + d) // count
        receives = (me - d + count) // count
        pair = []
        for index, (src, dst) in enumerate(((s_send, s_recv), (a_send, a_recv))):
            copy = pltpu.make_async_remote_copy(
                src_ref=src.at[k],
                dst_ref=dst.at[k],
                send_sem=send_sem.at[index, k],
                recv_sem=recv_sem.at[index, k],
                device_id=target,
                device_id_type=pl.DeviceIdType.MESH,
            )
            pl.when(sends == 1)(copy.start)
            pair.append(copy)
        copies.append((sends, pair))
        for copy in pair:
            pl.when(receives == 1)(copy.wait_recv)
        far_s = s_recv[k].astype(jnp.float32)
        far_a = a_recv[k]
        if k == 0:
            out_ref[...] = jnp.where(me == 0, sin_ref[...], far_s)
            dec_acc[...] = jnp.where(me == 0, jnp.zeros_like(far_a), far_a)
        else:
            acc_s = out_ref[...]
            acc_a = dec_acc[...]
            out_ref[...] = jnp.where(me >= d, acc_a[:, None, :] * far_s + acc_s, acc_s)
            dec_acc[...] = jnp.where(me >= d, acc_a * far_a, acc_a)
    for sends, pair in copies:
        for copy in pair:
            pl.when(sends == 1)(copy.wait_send)


def entering_state(decay, end_state, state_in):
    count = lax.axis_size("seq")
    heads, rows, lanes = end_state.shape
    decay_rows = jnp.broadcast_to(decay[:, None], (heads, lanes))
    shifts = [1]
    step = 1
    while step < count:
        shifts.append(step)
        step *= 2
    steps = len(shifts)
    return pl.pallas_call(
        functools.partial(scan_kernel, count, tuple(shifts)),
        out_shape=jax.ShapeDtypeStruct(end_state.shape, jnp.float32),
        in_specs=[pl.BlockSpec(memory_space=pltpu.VMEM)] * 3,
        out_specs=pl.BlockSpec(memory_space=pltpu.VMEM),
        scratch_shapes=[
            pltpu.VMEM(decay_rows.shape, jnp.float32),
            pltpu.VMEM((steps,) + end_state.shape, jnp.bfloat16),
            pltpu.VMEM((steps,) + decay_rows.shape, jnp.float32),
            pltpu.VMEM((steps,) + end_state.shape, jnp.bfloat16),
            pltpu.VMEM((steps,) + decay_rows.shape, jnp.float32),
            pltpu.SemaphoreType.DMA((2, steps)),
            pltpu.SemaphoreType.DMA((2, steps)),
        ],
        compiler_params=pltpu.CompilerParams(collective_id=0, has_side_effects=True),
    )(end_state, decay_rows, state_in)


def local(
    tokens,
    w_xz,
    w_bc,
    conv_x,
    conv_bc,
    tail_x,
    tail_bc,
    decay_code,
    skip_gain,
    state_in,
    norm_gain,
    w_out,
):
    rows = tokens.shape[0]
    heads, head_dim, nstate = state_in.shape
    inner = heads * head_dim
    seq_count = lax.axis_size("seq")
    first = lax.axis_index("seq") == 0
    w_x = w_xz[:, 0, :]
    w_z = w_xz[:, 1, :]
    heads_count = lax.axis_size("head")
    hindex = lax.axis_index("head")
    core = hindex % 2
    chip = hindex // 2
    chips = heads_count // 2
    width = w_bc.shape[1] // heads_count
    w_half = lax.dynamic_slice_in_dim(w_bc, hindex * width, width, axis=1)
    packed = jnp.concatenate([w_x, w_z, w_half], axis=1)
    gathered = lax.all_gather(packed, "seq", axis=0, tiled=True)
    w_out_cols = lax.all_gather(jnp.transpose(w_out), "seq", axis=0, tiled=True)
    lag = conv_x.shape[0] - 1
    earlier = passed_along(tokens[rows - lag :], "seq", 1)
    extended = jnp.concatenate([earlier, tokens], axis=0)
    xzbc = jnp.dot(extended, gathered, preferred_element_type=jnp.float32).astype(jnp.bfloat16)
    own_part = xzbc[:, 2 * inner :]
    other_part = lax.ppermute(own_part, "head", [(i, i ^ 1) for i in range(heads_count)])
    chip_piece = jnp.where(
        core == 0,
        jnp.concatenate([own_part, other_part], axis=1),
        jnp.concatenate([other_part, own_part], axis=1),
    )
    received = [chip_piece] + [
        lax.ppermute(chip_piece, "head", [(i, (i + 2 * k) % heads_count) for i in range(heads_count)])
        for k in range(1, chips)
    ]
    stacked = jnp.stack(received)
    bc_all = jnp.concatenate(
        [lax.dynamic_index_in_dim(stacked, (chip - j + chips) % chips, keepdims=False) for j in range(chips)],
        axis=1,
    )
    opening = lax.broadcasted_iota(jnp.int32, (rows + lag, 1), 0) < lag
    whole_x = jnp.where(first & opening, jnp.pad(tail_x, ((0, rows), (0, 0))), xzbc[:, :inner])
    whole_bc = jnp.where(first & opening, jnp.pad(tail_bc, ((0, rows), (0, 0))), bc_all)
    z_val = xzbc[lag:, inner : 2 * inner]
    x_conv = depthwise(whole_x, conv_x)
    bc_conv = depthwise(whole_bc, conv_bc)
    b_val = bc_conv[:, :nstate]
    c_val = bc_conv[:, nstate:]
    logdec = -decay_code.astype(jnp.float32) / (16.0 * rows * seq_count)
    blocks = rows // Q
    xb = x_conv.reshape(blocks, Q, heads, head_dim)
    bb = b_val.reshape(blocks, Q, nstate)
    cb = c_val.reshape(blocks, Q, nstate)
    cum = jnp.cumsum(logdec.reshape(blocks, Q, heads), axis=1)

    tail_decay = jnp.exp(cum[:, -1:, :] - cum)
    decayed_b = (
        jnp.transpose(tail_decay, (0, 2, 1))[..., None] * bb.astype(jnp.float32)[:, None]
    ).astype(jnp.bfloat16)
    added = jnp.einsum("bhsn,bshp->bhpn", decayed_b, xb, preferred_element_type=jnp.float32)
    block_decay = jnp.exp(cum[:, -1, :])
    before = [None]
    running = added[0]
    for b in range(1, blocks):
        before.append(running)
        running = block_decay[b][:, None, None] * running + added[b]
    cum_range = jnp.cumsum(logdec, axis=0)
    range_decay = jnp.exp(cum_range[-1])
    incoming = entering_state(range_decay, running, state_in)

    places = jnp.arange(Q)
    lower = places[:, None] >= places[None, :]
    cumt = jnp.transpose(cum, (0, 2, 1))
    diff = cumt[:, :, :, None] - cumt[:, :, None, :]
    decay = jnp.where(lower, jnp.exp(jnp.where(lower, diff, 0.0)), 0.0)
    scores = jnp.einsum("btn,bsn->bts", cb, bb, preferred_element_type=jnp.float32)
    weights = (decay * scores[:, None]).astype(jnp.bfloat16)
    parts = jnp.einsum("bhts,bshp->bthp", weights, xb, preferred_element_type=jnp.float32)
    pieces_out = [parts[0]]
    for b in range(1, blocks):
        carried = jnp.einsum(
            "tn,hpn->thp", cb[b].astype(jnp.float32), before[b], precision=lax.Precision.HIGHEST
        )
        pieces_out.append(parts[b] + carried * jnp.exp(cum[b])[:, :, None])
    parts = jnp.concatenate(pieces_out, axis=0)

    correction = jnp.einsum(
        "tn,hpn->thp", c_val.astype(jnp.float32), incoming, precision=lax.Precision.HIGHEST
    )
    parts = (parts + correction * jnp.exp(cum_range)[:, :, None]).reshape(rows, inner)
    y_val = parts / nstate + jnp.repeat(skip_gain, head_dim)[None, :] * x_conv.astype(jnp.float32)
    gated = y_val * jax.nn.silu(z_val.astype(jnp.float32))
    total_sq = lax.psum(jnp.sum(gated * gated, axis=1), "head")
    meansq = total_sq / (inner * lax.axis_size("head"))
    normed = (gated * lax.rsqrt(meansq[:, None] + 1e-05) * norm_gain[None, :]).astype(jnp.bfloat16)
    partial_t = lax.dot_general(
        w_out_cols, normed, (((1,), (1,)), ((), ())), preferred_element_type=jnp.float32
    )
    return jnp.transpose(
        lax.psum_scatter(partial_t.astype(jnp.bfloat16), "head", scatter_dimension=0, tiled=True)
    )


def solution(mesh):
    return jax.shard_map(
        local,
        mesh=mesh,
        in_specs=(
            P("seq", None),
            P("seq", None, "head"),
            P("seq", None),
            P(None, "head"),
            P(),
            P(None, "head"),
            P(),
            P("seq", "head"),
            P("head"),
            P("head", None, None),
            P("head"),
            P("head", "seq"),
        ),
        out_specs=P("seq", "head"),
        check_vma=False,
    )
```
